128 devices in a mesh: seq: 32 (over z, x, core), head: 4 (over y).
Axes of the slice: x: 4, y: 4, z: 4, core: 2. Of those that a mesh axis runs over, the one named last changes fastest.
Arguments:
- hidden: bfloat16 [8192, 2048], P('seq'), may hold values from -6 to 6
- w_query: bfloat16 [2048, 2048], P(None, 'head'), may hold values from -0.125 to 0.125
- w_key: bfloat16 [2048, 2048], P(None, 'head'), as said below
- w_value: bfloat16 [2048, 4096], P(None, 'head'), may hold values from -0.125 to 0.125
- w_gate: bfloat16 [2048, 4096], P(None, 'head'), may hold values from -0.125 to 0.125
- w_beta: bfloat16 [2048, 32], P(None, 'head'), may hold values from -0.125 to 0.125
- conv_query: bfloat16 [4, 2048], P(None, 'head'), may hold values from -3 to 3
- conv_key: bfloat16 [4, 2048], P(None, 'head'), may hold values from -3 to 3
- conv_value: bfloat16 [4, 4096], P(None, 'head'), may hold values from -3 to 3
- norm_gain: bfloat16 [128], replicated, may hold values from 0.5 to 1.5
- w_out: bfloat16 [4096, 2048], P('head'), may hold values from -0.09375 to 0.09375
Outputs:
- mixed: bfloat16 [8192, 2048], P('seq', 'head')
The draws below stay inside these ranges and needn't reach their ends.
Inputs may be any that keep to these rules, and one draw needn't show every extreme that they name: `w_key`: entries of the key projection.
All inputs are finite; a program needn't handle non-finite values.
Results may differ from the reference program's by a relative error of at most 0.017.
Values may be sent and summed in bfloat16 or wider, within the bound.
A program may use at most 128 MiB of HBM per device.

```python
import jax
import jax.numpy as jnp
from jax import lax

D = 2048
HK = 16
HV = 32
DK = 128
DV = 128
KER = 4
SPAN = 64
TOKENS = 8192
N_HEAD = 4


def draw_w_key(key, part):
    first_key, second_key = jax.random.split(jax.random.fold_in(key, 17))
    base_vals = jnp.clip(jax.random.normal(first_key, (D, HK * DK), jnp.float32), -6.0, 6.0)
    exponent = jax.random.uniform(second_key, (HK * DK,), jnp.float32, -2.0, 0.0)
    return (base_vals * jnp.power(10.0, exponent)[None, :] / jnp.sqrt(jnp.float32(D))).astype(jnp.bfloat16)


def levels(rng, extent, cuts, smallest, largest):
    loudness, own = 1.0, jax.random.fold_in(rng, 6)
    for axis_at, parts in cuts:
        heights = jnp.exp(jax.random.uniform(jax.random.fold_in(own, axis_at), (parts,), jnp.float32, smallest / len(cuts), largest / len(cuts)))
        loudness = loudness * jnp.repeat(heights, extent[axis_at] // parts).reshape([-1 if axis == axis_at else 1 for axis in range(len(extent))])
    return loudness


def centred(rng, shape, deviation, reach, cuts=(), kind=jnp.bfloat16):
    drawn = jax.random.normal(rng, shape, jnp.float32) * deviation
    if len(cuts) > 0:
        drawn = levels(rng, shape, cuts, -0.22, 0.18) * drawn
    return jnp.clip(drawn, min=-reach, max=reach).astype(kind)


def setup_inputs(seed: int = 0) -> dict:
    seeds = jax.random.split(jax.random.key(seed), 12)
    hidden = centred(seeds[0], (TOKENS, D), 1.0, 6.0, ((0, 32),))
    w_query = centred(seeds[1], (D, HK * DK), D ** -0.5, 0.125, ((1, 4),))
    w_key = draw_w_key(jax.random.fold_in(seeds[11], 71), 0)
    w_value = centred(seeds[3], (D, HV * DV), D ** -0.5, 0.125, ((1, 4),))
    w_gate = centred(seeds[4], (D, HV * DV), D ** -0.5, 0.125, ((1, 4),))
    w_beta = centred(seeds[5], (D, HV), D ** -0.5, 0.125, ((1, 4),))
    conv_query = centred(seeds[6], (KER, HK * DK), 0.5, 3.0, ((1, 4),))
    conv_key = centred(seeds[7], (KER, HK * DK), 0.5, 3.0, ((1, 4),))
    conv_value = centred(seeds[8], (KER, HV * DV), 0.5, 3.0, ((1, 4),))
    norm_gain = jnp.clip(1.0 + 0.1 * jax.random.normal(seeds[9], (DV,), jnp.float32), 0.5, 1.5).astype(jnp.bfloat16)
    w_out = centred(seeds[10], (HV * DV, D), (HV * DV) ** -0.5, 0.09375, ((0, 4),))
    return dict(hidden=hidden, w_query=w_query, w_key=w_key, w_value=w_value, w_gate=w_gate, w_beta=w_beta, conv_query=conv_query, conv_key=conv_key, conv_value=conv_value, norm_gain=norm_gain, w_out=w_out)


exact_mode = lax.Precision.HIGHEST
eps_norm = 1e-06

def contract(form, left, right):
    return jnp.einsum(form, left, right, precision=exact_mode)

def unit_rows(values):
    return values * lax.rsqrt(lax.optimization_barrier(jnp.sum(values * values, axis=-1, keepdims=True)) + eps_norm)

def convolve(projected, rim_rows, kernel):
    padded = jnp.concatenate([rim_rows, projected], axis=0).astype(jnp.float32)
    count_rows = projected.shape[0]
    summed = jnp.zeros((count_rows, projected.shape[1]), jnp.float32)
    for offset in range(KER):
        summed = summed + kernel[offset].astype(jnp.float32) * padded[offset:offset + count_rows]
    return jax.nn.silu(summed)

def delta_block(state_now, inputs):
    queries, key_act, values, beta_gate = inputs
    size_block = key_act.shape[1]
    key_gram = contract('hcd,hed->hce', key_act, key_act)
    below = jnp.tril(jnp.ones((size_block, size_block), jnp.float32), -1)
    unit_diag = jnp.eye(size_block, dtype=jnp.float32)
    system = unit_diag + beta_gate[:, :, None] * key_gram * below
    solved_keys = lax.linalg.triangular_solve(system, beta_gate[:, :, None] * key_act, left_side=True, lower=True)
    solved_values = lax.linalg.triangular_solve(system, beta_gate[:, :, None] * values, left_side=True, lower=True)
    updates = solved_values - contract('hcd,hvd->hcv', solved_keys, state_now)
    attend = contract('hcd,hed->hce', queries, key_act) * (below + unit_diag)
    outputs = contract('hcd,hvd->hcv', queries, state_now) + contract('hce,hev->hcv', attend, updates)
    state_next = state_now + contract('hcv,hcd->hvd', updates, key_act)
    return (state_next, outputs)

def delta_pass(queries, key_act, values, beta_gate, state_start):
    count_rows = queries.shape[0]
    blocks = count_rows // SPAN

    def arrange(array):
        return jnp.moveaxis(array.reshape((blocks, SPAN) + array.shape[1:]), 1, 2)
    return lax.scan(delta_block, state_start, (arrange(queries), arrange(key_act), arrange(values), arrange(beta_gate)))

def reference(hidden, w_query, w_key, w_value, w_gate, w_beta, conv_query, conv_key, conv_value, norm_gain, w_out):
    q_proj = jnp.dot(hidden.astype(jnp.float32), w_query.astype(jnp.float32), preferred_element_type=jnp.float32).astype(jnp.bfloat16)
    k_proj = jnp.dot(hidden.astype(jnp.float32), w_key.astype(jnp.float32), preferred_element_type=jnp.float32).astype(jnp.bfloat16)
    v_proj = jnp.dot(hidden.astype(jnp.float32), w_value.astype(jnp.float32), preferred_element_type=jnp.float32).astype(jnp.bfloat16)
    gate_proj = jnp.dot(hidden.astype(jnp.float32), w_gate.astype(jnp.float32), preferred_element_type=jnp.float32).astype(jnp.bfloat16)
    beta_gate = 0.05 + 0.15 * jax.nn.sigmoid(jnp.dot(hidden.astype(jnp.float32), w_beta.astype(jnp.float32), preferred_element_type=jnp.float32))
    key_zeros = jnp.zeros((KER - 1, HK * DK), jnp.bfloat16)
    value_zeros = jnp.zeros((KER - 1, HV * DV), jnp.bfloat16)
    queries = unit_rows(convolve(q_proj, key_zeros, conv_query).reshape(TOKENS, HK, DK))
    key_act = unit_rows(convolve(k_proj, key_zeros, conv_key).reshape(TOKENS, HK, DK))
    values = convolve(v_proj, value_zeros, conv_value).reshape(TOKENS, HV, DV)
    group_size = HV // HK
    queries = jnp.repeat(queries, group_size, axis=1)
    key_act = jnp.repeat(key_act, group_size, axis=1)
    state_start = jnp.zeros((HV, DV, DK), jnp.float32)
    state_end, outputs = delta_pass(queries, key_act, values, beta_gate, state_start)
    attended = jnp.moveaxis(outputs, 2, 1).reshape(TOKENS, HV, DV)
    scale_rms = lax.rsqrt(lax.optimization_barrier(jnp.mean(attended * attended, axis=-1, keepdims=True)) + eps_norm)
    gate_act = jax.nn.silu(gate_proj.astype(jnp.float32).reshape(TOKENS, HV, DV))
    normed = attended * scale_rms * norm_gain.astype(jnp.float32) * gate_act
    gated = normed.reshape(TOKENS, HV * DV).astype(jnp.bfloat16)
    width_group = HV * DV // N_HEAD
    mixed = jnp.zeros((TOKENS, D), jnp.float32)
    for group_index in range(N_HEAD):
        lo_col = group_index * width_group
        partial_sum = jnp.dot(gated[:, lo_col:lo_col + width_group].astype(jnp.float32), w_out[lo_col:lo_col + width_group].astype(jnp.float32), preferred_element_type=jnp.float32)
        mixed = mixed + partial_sum.astype(jnp.bfloat16).astype(jnp.float32)
    return mixed.astype(jnp.bfloat16)
```

```python
import functools

import jax
import jax.numpy as jnp
from jax import lax
from jax.experimental import pallas as pl
from jax.experimental.pallas import tpu as pltpu
from jax.sharding import PartitionSpec as P

DK = 128
DV = 128
KER = 4
HALO = 16
eps_norm = 1e-06
F32 = jnp.float32
BF16 = jnp.bfloat16
MESH = pl.DeviceIdType.MESH


def mm(a, b):
    return jnp.dot(a, b, preferred_element_type=F32)


def mm_nt(a, b):
    return lax.dot_general(a, b, (((1,), (1,)), ((), ())), preferred_element_type=F32)


def mm_tn(a, b):
    return lax.dot_general(a, b, (((0,), (0,)), ((), ())), preferred_element_type=F32)


def silu(x):
    return x / (1.0 + jnp.exp(-x))


def unit_rows(x):
    return x * lax.rsqrt(jnp.sum(x * x, axis=-1, keepdims=True) + eps_norm)


def block_solve(systems, row, col):
    eye = (row == col).astype(F32)
    same = (row // 16) == (col // 16)
    low = [a.astype(BF16) for a in systems]
    powers = [jnp.where(same, -a, 0.0) for a in systems]
    solved = [eye + n for n in powers]
    powers = [n.astype(BF16) for n in powers]
    for _ in range(3):
        powers = [mm(n, n).astype(BF16) for n in powers]
        solved = [x + mm(x.astype(BF16), n) for x, n in zip(solved, powers)]
    size = 16
    while size < row.shape[0]:
        off = ((row // (2 * size)) == (col // (2 * size))) & ((row // size) != (col // size))
        rounded = [x.astype(BF16) for x in solved]
        cross = [mm(jnp.where(off, a, 0.0).astype(BF16), x).astype(BF16) for a, x in zip(low, rounded)]
        solved = [s - mm(x, c) for s, x, c in zip(solved, rounded, cross)]
        size *= 2
    return [x.astype(BF16) for x in solved]


def local_delta(queries, keys, values, betas):
    rows = queries.shape[0]
    row = lax.broadcasted_iota(jnp.int32, (rows, rows), 0)
    col = lax.broadcasted_iota(jnp.int32, (rows, rows), 1)
    qb, kb = queries.astype(BF16), keys.astype(BF16)
    gram = jnp.where(row > col, mm_nt(kb, kb), 0.0)
    attend = jnp.where(row >= col, mm_nt(qb, kb), 0.0).astype(BF16)
    inverses = block_solve([b * gram for b in betas], row, col)
    results = []
    for inv, b, v in zip(inverses, betas, values):
        sides = jnp.concatenate([b * keys, b * v], axis=1).astype(BF16)
        both = mm(inv, sides).astype(BF16)
        carry = mm_tn(kb, both)
        seen = mm(attend, both)
        results.append((seen[:, DK:], queries - seen[:, :DK], carry))
    return results


def local_kernel(hid, halo, wq, wk, wv, wb, cq, ck, cv, part_ref, ask_ref, carry_ref, ext_ref):
    rows = hid.shape[0]
    step = pl.program_id(0)
    h = hid[...]
    edge = halo[...]

    def project(w, taps):
        weights = w[...]
        width = weights.shape[1]
        ext_ref[:8, :width] = mm(edge, weights).astype(BF16).astype(F32)[HALO - 8 :]
        ext_ref[8:, :width] = mm(h, weights).astype(BF16).astype(F32)
        t = taps[...].astype(F32)
        summed = jnp.zeros((rows, width), F32)
        for j in range(KER):
            summed = summed + t[j : j + 1] * ext_ref[pl.ds(8 - KER + 1 + j, rows), :width]
        return silu(summed)

    queries = unit_rows(project(wq, cq))
    keys = unit_rows(project(wk, ck))
    values = project(wv, cv)
    group = values.shape[1] // DV
    beta = 0.05 + 0.15 / (1.0 + jnp.exp(-mm(h, wb[...])))
    lane = lax.broadcasted_iota(jnp.int32, beta.shape, 1)
    betas = [
        jnp.sum(jnp.where(lane == step * group + j, beta, 0.0), axis=1, keepdims=True)
        for j in range(group)
    ]
    parts = [values[:, j * DV : (j + 1) * DV] for j in range(group)]
    for j, (part, ask, carry) in enumerate(local_delta(queries, keys, parts, betas)):
        part_ref[:, j * DV : (j + 1) * DV] = part
        ask_ref[:, j * DV : (j + 1) * DV] = ask.astype(BF16)
        carry_ref[j] = carry.astype(BF16)


def local_call(hidden, halo, w_query, w_key, w_value, w_beta, c_query, c_key, c_value):
    rows, depth = hidden.shape
    heads_key = w_query.shape[1] // DK
    heads = w_value.shape[1] // DV
    group = heads // heads_key
    wide = group * DV
    whole = lambda shape: pl.BlockSpec(shape, lambda g: (0, 0))
    cols = lambda r, c: pl.BlockSpec((r, c), lambda g: (0, g))
    return pl.pallas_call(
        local_kernel,
        grid=(heads_key,),
        in_specs=[
            whole((rows, depth)),
            whole((HALO, depth)),
            cols(depth, DK),
            cols(depth, DK),
            cols(depth, wide),
            whole((depth, heads)),
            cols(KER, DK),
            cols(KER, DK),
            cols(KER, wide),
        ],
        out_specs=[
            cols(rows, wide),
            cols(rows, wide),
            pl.BlockSpec((group, DK, DK + DV), lambda g: (g, 0, 0)),
        ],
        out_shape=[
            jax.ShapeDtypeStruct((rows, heads * DV), F32),
            jax.ShapeDtypeStruct((rows, heads * DV), BF16),
            jax.ShapeDtypeStruct((heads, DK, DK + DV), BF16),
        ],
        scratch_shapes=[pltpu.VMEM((rows + 8, wide), F32)],
        name="local_rule",
    )(hidden, halo, w_query, w_key, w_value, w_beta, c_query, c_key, c_value)


def join(first, second):
    return first + second - mm(second[:, :DK].astype(BF16), first.astype(BF16))


def carry_kernel(
    members, groups, carry_ref, state_ref, got, total, total_got, start, s1, r1, s2, r2, s3, r3
):
    me = lax.axis_index("seq")
    slot = lax.rem(me, members)
    team = me // members
    barrier = pltpu.get_barrier_semaphore()
    peers = [team * members + lax.rem(slot + d, members) for d in range(1, members)]
    mates = [lax.rem(team + d, groups) * members + slot for d in range(1, groups)]
    for peer in peers + mates:
        pl.semaphore_signal(barrier, inc=1, device_id={"seq": peer}, device_id_type=MESH)
    pl.semaphore_wait(barrier, len(peers) + len(mates))

    def remote(src, dst, send, recv, peer):
        return pltpu.make_async_remote_copy(
            src_ref=src,
            dst_ref=dst,
            send_sem=send,
            recv_sem=recv,
            device_id={"seq": peer},
            device_id_type=MESH,
        )

    sends = []
    for d in range(1, members):
        to = lax.rem(slot + d, members)
        copy = remote(carry_ref.at[to], got.at[slot], s1.at[d], r1.at[slot], peers[d - 1])
        copy.start()
        sends.append(copy)
    got[slot] = carry_ref[slot]
    prefix = []
    running = None
    for i in range(members):

        @pl.when(slot != i)
        def _():
            remote(got.at[i], got.at[i], s1.at[0], r1.at[i], peers[0]).wait_recv()

        mine = got[i].astype(F32)
        prefix.append(running)
        running = mine if running is None else join(running, mine)
    total[...] = running.astype(BF16)
    for d in range(1, groups):
        copy = remote(total, total_got.at[team], s2.at[d], r2.at[team], mates[d - 1])
        copy.start()
        sends.append(copy)
    total_got[team] = running.astype(BF16)
    state = jnp.zeros((DK, DV), F32)
    entry = state
    for i in range(groups):

        @pl.when(team != i)
        def _():
            remote(total_got.at[i], total_got.at[i], s2.at[0], r2.at[i], mates[0]).wait_recv()

        entry = jnp.where(team == i, state, entry)
        if i < groups - 1:
            whole = total_got[i].astype(F32)
            state = state + whole[:, DK:] - mm(whole[:, :DK].astype(BF16), state.astype(BF16))
    rounded = entry.astype(BF16)
    for i in range(members):
        begin = entry
        if i > 0:
            begin = entry + prefix[i][:, DK:] - mm(prefix[i][:, :DK].astype(BF16), rounded)
        start[i] = begin.astype(BF16)
    for d in range(1, members):
        to = lax.rem(slot + d, members)
        copy = remote(start.at[to], state_ref.at[slot], s3.at[d], r3.at[slot], peers[d - 1])
        copy.start()
        sends.append(copy)
    state_ref[slot] = start[slot]
    for i in range(members):

        @pl.when(slot != i)
        def _():
            remote(state_ref.at[i], state_ref.at[i], s3.at[0], r3.at[i], peers[0]).wait_recv()

    for copy in sends:
        copy.wait_send()


def carry_call(carry, size_seq):
    heads = carry.shape[0]
    members, groups = heads, size_seq // heads
    dma = pltpu.SemaphoreType.DMA
    return pl.pallas_call(
        functools.partial(carry_kernel, members, groups),
        in_specs=[pl.BlockSpec(memory_space=pltpu.VMEM)],
        out_specs=pl.BlockSpec(memory_space=pltpu.VMEM),
        out_shape=jax.ShapeDtypeStruct((heads, DK, DV), BF16),
        scratch_shapes=[
            pltpu.VMEM((members, DK, DK + DV), BF16),
            pltpu.VMEM((DK, DK + DV), BF16),
            pltpu.VMEM((groups, DK, DK + DV), BF16),
            pltpu.VMEM((members, DK, DV), BF16),
            dma((members,)),
            dma((members,)),
            dma((groups,)),
            dma((groups,)),
            dma((members,)),
            dma((members,)),
        ],
        compiler_params=pltpu.CompilerParams(collective_id=0, has_side_effects=True),
        name="carry_scan",
    )(carry)


def gated_kernel(part_ref, ask_ref, state_ref, gate_ref, gain_ref, w_ref, out_ref, gated_ref):
    @pl.when(pl.program_id(0) == 0)
    def _():
        gain = gain_ref[...].astype(F32)
        for i in range(state_ref.shape[0]):
            at = slice(i * DV, (i + 1) * DV)
            attended = part_ref[:, at] + mm(ask_ref[:, at], state_ref[i])
            scale = lax.rsqrt(jnp.mean(attended * attended, axis=-1, keepdims=True) + eps_norm)
            gate = silu(gate_ref[:, at].astype(F32))
            gated_ref[:, at] = (attended * scale * gain * gate).astype(BF16)

    out_ref[0] = mm(gated_ref[...], w_ref[...]).astype(BF16)


def gated_call(part, ask, state, gate, gain, w_out, size_head):
    rows, wide = part.shape
    heads = state.shape[0]
    tile = w_out.shape[1] // size_head
    return pl.pallas_call(
        gated_kernel,
        grid=(size_head,),
        in_specs=[
            pl.BlockSpec((rows, wide), lambda n: (0, 0)),
            pl.BlockSpec((rows, wide), lambda n: (0, 0)),
            pl.BlockSpec((heads, DK, DV), lambda n: (0, 0, 0)),
            pl.BlockSpec((rows, wide), lambda n: (0, 0)),
            pl.BlockSpec((1, DV), lambda n: (0, 0)),
            pl.BlockSpec((wide, tile), lambda n: (0, n)),
        ],
        out_specs=pl.BlockSpec((1, rows, tile), lambda n: (n, 0, 0)),
        out_shape=jax.ShapeDtypeStruct((size_head, rows, tile), BF16),
        scratch_shapes=[pltpu.VMEM((rows, wide), BF16)],
        name="gated_out",
    )(part, ask, state, gate, gain, w_out)


def shares_kernel(count, part_ref, out_ref, got, send, recv):
    me = lax.axis_index("head")
    barrier = pltpu.get_barrier_semaphore()
    peers = [lax.rem(me + d, count) for d in range(1, count)]
    for peer in peers:
        pl.semaphore_signal(barrier, inc=1, device_id={"head": peer}, device_id_type=MESH)
    pl.semaphore_wait(barrier, count - 1)
    copies = []
    for d in range(1, count):
        copy = pltpu.make_async_remote_copy(
            src_ref=part_ref.at[peers[d - 1]],
            dst_ref=got.at[d],
            send_sem=send.at[d],
            recv_sem=recv.at[d],
            device_id={"head": peers[d - 1]},
            device_id_type=MESH,
        )
        copy.start()
        copies.append(copy)
    total = part_ref[me].astype(F32)
    for d in range(1, count):
        copies[d - 1].wait_recv()
        total = total + got[d].astype(F32)
    out_ref[...] = total.astype(BF16)
    for copy in copies:
        copy.wait_send()


def shares_call(part):
    count, rows, tile = part.shape
    return pl.pallas_call(
        functools.partial(shares_kernel, count),
        in_specs=[pl.BlockSpec(memory_space=pltpu.VMEM)],
        out_specs=pl.BlockSpec(memory_space=pltpu.VMEM),
        out_shape=jax.ShapeDtypeStruct((rows, tile), BF16),
        scratch_shapes=[
            pltpu.VMEM((count, rows, tile), BF16),
            pltpu.SemaphoreType.DMA((count,)),
            pltpu.SemaphoreType.DMA((count,)),
        ],
        compiler_params=pltpu.CompilerParams(collective_id=1, has_side_effects=True),
        name="share_sum",
    )(part)


def shards(
    hidden,
    w_query,
    w_key,
    w_value,
    w_gate,
    w_beta,
    conv_query,
    conv_key,
    conv_value,
    norm_gain,
    w_out,
):
    rows = hidden.shape[0]
    size_seq = lax.axis_size("seq")
    halo = lax.ppermute(
        hidden[rows - HALO :], "seq", [(i, i + 1) for i in range(size_seq - 1)]
    )
    gate = jnp.dot(hidden, w_gate, preferred_element_type=F32).astype(BF16)
    part, ask, carry = local_call(
        hidden, halo, w_query, w_key, w_value, w_beta, conv_query, conv_key, conv_value
    )
    state = carry_call(carry, size_seq)
    partial = gated_call(
        part, ask, state, gate, norm_gain.reshape(1, DV), w_out, lax.axis_size("head")
    )
    return shares_call(partial)


def solution(mesh):
    in_specs = (
        P("seq", None),
        P(None, "head"),
        P(None, "head"),
        P(None, "head"),
        P(None, "head"),
        P(None, "head"),
        P(None, "head"),
        P(None, "head"),
        P(None, "head"),
        P(),
        P("head", None),
    )
    out_specs = P("seq", "head")
    return jax.shard_map(shards, mesh=mesh, in_specs=in_specs, out_specs=out_specs, check_vma=False)
```

```python
import functools

import jax
import jax.numpy as jnp
from jax import lax
from jax.experimental import pallas as pl
from jax.experimental.pallas import tpu as pltpu
from jax.sharding import PartitionSpec as P

DK = 128
DV = 128
KER = 4
HALO = 16
eps_norm = 1e-06
F32 = jnp.float32
BF16 = jnp.bfloat16
MESH = pl.DeviceIdType.MESH


def mm(a, b):
    return jnp.dot(a, b, preferred_element_type=F32)


def mm_nt(a, b):
    return lax.dot_general(a, b, (((1,), (1,)), ((), ())), preferred_element_type=F32)


def mm_tn(a, b):
    return lax.dot_general(a, b, (((0,), (0,)), ((), ())), preferred_element_type=F32)


def sigmoid(x):
    return 0.5 + 0.5 * jnp.tanh(0.5 * x)


def silu(x):
    half = 0.5 * x
    return half + half * jnp.tanh(half)


def unit_rows(x):
    return x * lax.rsqrt(jnp.sum(x * x, axis=-1, keepdims=True) + eps_norm)


def block_solve(systems, rounded, row, col):
    eye = (row == col).astype(F32)
    same = (row // 16) == (col // 16)
    powers = [jnp.where(same, -a, 0.0) for a in systems]
    solved = [eye + n for n in powers]
    powers = [n.astype(BF16) for n in powers]
    for _ in range(3):
        powers = [mm(n, n).astype(BF16) for n in powers]
        solved = [x + mm(x.astype(BF16), n) for x, n in zip(solved, powers)]
    size = 16
    while size < row.shape[0]:
        off = ((row // (2 * size)) == (col // (2 * size))) & ((row // size) != (col // size))
        halves = [x.astype(BF16) for x in solved]
        zero = jnp.zeros((), BF16)
        cross = [mm(jnp.where(off, a, zero), x).astype(BF16) for a, x in zip(rounded, halves)]
        solved = [s - mm(x, c) for s, x, c in zip(solved, halves, cross)]
        size *= 2
    return [x.astype(BF16) for x in solved]


def local_delta(queries, keys, values, betas):
    rows = queries[0].shape[0]
    half = rows // 2
    row = lax.broadcasted_iota(jnp.int32, (half, half), 0)
    col = lax.broadcasted_iota(jnp.int32, (half, half), 1)
    qb = [q.astype(BF16) for q in queries]
    kb = [k.astype(BF16) for k in keys]
    grams = [mm_nt(k, k) for k in kb]
    scores = [mm_nt(q, k) for q, k in zip(qb, kb)]
    systems, corners = [], []
    for gram, many in zip(grams, betas):
        first = jnp.where(row > col, gram[:half, :half], 0.0)
        last = jnp.where(row > col, gram[half:, half:], 0.0)
        for b in many:
            systems += [b[:half] * first, b[half:] * last]
            corners.append((b[half:] * gram[half:, :half]).astype(BF16))
    inverses = block_solve(systems, [a.astype(BF16) for a in systems], row, col)
    sides = []
    for k, vs, bs in zip(keys, values, betas):
        sides += [jnp.concatenate([b * k, b * v], axis=1) for b, v in zip(bs, vs)]
    tops = [mm(x, s[:half].astype(BF16)).astype(BF16) for x, s in zip(inverses[::2], sides)]
    rest = [(s[half:] - mm(c, t)).astype(BF16) for s, c, t in zip(sides, corners, tops)]
    ends = [mm(x, r).astype(BF16) for x, r in zip(inverses[1::2], rest)]
    results = []
    at = 0
    for q, k, score, many in zip(queries, kb, scores, betas):
        upper = jnp.where(row >= col, score[:half, :half], 0.0).astype(BF16)
        lower = jnp.concatenate(
            [score[half:, :half], jnp.where(row >= col, score[half:, half:], 0.0)], axis=1
        ).astype(BF16)
        for _ in many:
            both = jnp.concatenate([tops[at], ends[at]], axis=0)
            carry = mm_tn(k, both)
            seen = jnp.concatenate([mm(upper, tops[at]), mm(lower, both)], axis=0)
            results.append((seen[:, DK:], q - seen[:, :DK], carry))
            at += 1
    return results


def join(first, second):
    return first + second - mm(second[:, :DK].astype(BF16), first.astype(BF16))


def layer_kernel(
    sizes, hid, wq, wk, wv, wg, wb, cq, ck, cv, gain, wo, out_ref, bufs, rule, scan, shares
):
    size_seq, size_head, members = sizes
    groups = size_seq // members
    me, row_at = lax.axis_index("seq"), lax.axis_index("head")
    slot, team = lax.rem(me, members), me // members
    after, before = lax.rem(me + 1, size_seq), lax.rem(me + size_seq - 1, size_seq)
    peers = [team * members + lax.rem(slot + d, members) for d in range(1, members)]
    mates = [lax.rem(team + d, groups) * members + slot for d in range(1, groups)]
    others = [lax.rem(row_at + d, size_head) for d in range(1, size_head)]

    def remote(src, dst, send, recv, to):
        return pltpu.make_async_remote_copy(
            src_ref=src, dst_ref=dst, send_sem=send, recv_sem=recv, device_id=to, device_id_type=MESH
        )

    h_buf, q_buf, k_buf, v_buf, g_buf, o_buf, halo, load_sem, edge_send, edge_recv = bufs
    loads = []
    for i, (src, dst) in enumerate(
        ((hid, h_buf), (wq, q_buf), (wk, k_buf), (wv, v_buf), (wg, g_buf), (wo, o_buf))
    ):
        copy = pltpu.make_async_copy(src, dst, load_sem.at[i])
        copy.start()
        loads.append(copy)

    barrier = pltpu.get_barrier_semaphore()
    greeted = [{"seq": i} for i in [after, before] + peers + mates]
    greeted += [{"head": i} for i in (others[0], others[-1])]
    for to in greeted:
        pl.semaphore_signal(barrier, inc=1, device_id=to, device_id_type=MESH)
    pl.semaphore_wait(barrier, len(greeted))

    rows = h_buf.shape[0]
    edge = remote(hid.at[pl.ds(rows - HALO, HALO)], halo, edge_send, edge_recv, {"seq": after})
    edge.start()

    ext_ref, part_ref, ask_ref, carry_ref = rule
    loads[0].wait()
    h = h_buf[...]
    beta = 0.05 + 0.15 * sigmoid(mm_nt(h, wb[...]))
    lane = lax.broadcasted_iota(jnp.int32, beta.shape, 1)
    betas = [
        jnp.sum(jnp.where(lane == j, beta, 0.0), axis=1, keepdims=True)
        for j in range(beta.shape[1])
    ]
    edge.wait_recv()
    border = halo[...]
    tall = jnp.concatenate([jnp.where(me > 0, border, jnp.zeros_like(border)), h], axis=0)

    def project(load, w, taps):
        load.wait()
        width = w.shape[1]
        ext_ref[:, :width] = mm(tall, w[...]).astype(BF16).astype(F32)[HALO - 8 :]
        t = taps[...].astype(F32)
        summed = jnp.zeros((rows, width), F32)
        for j in range(KER):
            summed = summed + t[j : j + 1] * ext_ref[pl.ds(8 - KER + 1 + j, rows), :width]
        return silu(summed)

    split = lambda x: [x[:, j * DK : (j + 1) * DK] for j in range(x.shape[1] // DK)]
    queries = [unit_rows(x) for x in split(project(loads[1], q_buf, cq))]
    keys = [unit_rows(x) for x in split(project(loads[2], k_buf, ck))]
    values = split(project(loads[3], v_buf, cv))
    heads = len(values)
    group = heads // len(keys)
    nest = lambda x: [x[j : j + group] for j in range(0, len(x), group)]
    for j, (part, ask, carry) in enumerate(
        local_delta(queries, keys, nest(values), nest(betas))
    ):
        part_ref[:, j * DV : (j + 1) * DV] = part
        ask_ref[:, j * DV : (j + 1) * DV] = ask.astype(BF16)
        carry_ref[j] = carry.astype(BF16)

    got, total, total_got, start, state_ref, s1, r1, s2, r2, s3, r3 = scan
    sends = []
    for d in range(1, members):
        to = lax.rem(slot + d, members)
        copy = remote(carry_ref.at[to], got.at[slot], s1.at[d], r1.at[slot], {"seq": peers[d - 1]})
        copy.start()
        sends.append(copy)
    got[slot] = carry_ref[slot]

    gate_ref, gated_ref, keep, relay, opp, direct, hop, land, sr, rr = shares
    loads[4].wait()
    gain_row = gain[...].astype(F32)
    gate = silu(mm(h, g_buf[...]).astype(BF16).astype(F32))
    for j in range(heads):
        at = slice(j * DV, (j + 1) * DV)
        gate_ref[:, at] = gate[:, at] * gain_row

    prefix = []
    running = None
    for i in range(members):

        @pl.when(slot != i)
        def _():
            remote(got.at[i], got.at[i], s1.at[0], r1.at[i], {"seq": peers[0]}).wait_recv()

        mine = got[i].astype(F32)
        prefix.append(running)
        running = mine if running is None else join(running, mine)
    total[...] = running.astype(BF16)
    for d in range(1, groups):

        @pl.when(team + d < groups)
        def _():
            remote(
                total, total_got.at[team], s2.at[d], r2.at[team], {"seq": mates[d - 1]}
            ).start()

    state = jnp.zeros((DK, DV), F32)
    entry = state
    for i in range(groups - 1):

        @pl.when(team > i)
        def _():
            remote(total_got.at[i], total_got.at[i], s2.at[0], r2.at[i], {"seq": mates[0]}).wait_recv()

        whole = total_got[i].astype(F32)
        moved = state + whole[:, DK:] - mm(whole[:, :DK].astype(BF16), state.astype(BF16))
        state = jnp.where(team > i, moved, state)
    entry = state
    rounded = entry.astype(BF16)
    for i in range(members):
        begin = entry
        if i > 0:
            begin = entry + prefix[i][:, DK:] - mm(prefix[i][:, :DK].astype(BF16), rounded)
        start[i] = begin.astype(BF16)
    for d in range(1, members):
        to = lax.rem(slot + d, members)
        copy = remote(
            start.at[to], state_ref.at[slot], s3.at[d], r3.at[slot], {"seq": peers[d - 1]}
        )
        copy.start()
        sends.append(copy)
    state_ref[slot] = start[slot]
    for i in range(members):

        @pl.when(slot != i)
        def _():
            remote(state_ref.at[i], state_ref.at[i], s3.at[0], r3.at[i], {"seq": peers[0]}).wait_recv()

        at = slice(i * DV, (i + 1) * DV)
        attended = part_ref[:, at] + mm(ask_ref[:, at], state_ref[i])
        scale = lax.rsqrt(jnp.mean(attended * attended, axis=-1, keepdims=True) + eps_norm)
        gated_ref[:, at] = (attended * scale * gate_ref[:, at]).astype(BF16)

    loads[5].wait()
    gated = gated_ref[...]
    tile = out_ref.shape[1]
    half = rows // 2
    upper, lower = pl.ds(0, half), pl.ds(half, half)

    def share(to):
        columns = pl.ds(pl.multiple_of(to * tile, tile), tile)
        return mm(gated, o_buf[:, columns]).astype(BF16)

    right, far, left = others
    opp[...] = share(far)
    hops = [
        remote(opp.at[upper], hop.at[upper], sr.at[0], rr.at[0], {"head": right}),
        remote(opp.at[lower], hop.at[lower], sr.at[1], rr.at[1], {"head": left}),
    ]
    for copy in hops:
        copy.start()
    to_right, to_left = share(right), share(left)
    keep[upper], keep[lower] = to_right[:half], to_left[half:]
    direct[lower], direct[upper] = to_right[half:], to_left[:half]
    lands = [
        remote(direct.at[lower], land.at[lower], sr.at[2], rr.at[2], {"head": right}),
        remote(direct.at[upper], land.at[upper], sr.at[3], rr.at[3], {"head": left}),
    ]
    for copy in lands:
        copy.start()
    ends = []
    for n, (at, to) in enumerate(((upper, right), (lower, left))):
        hops[n].wait_recv()
        relay[at] = (hop[at].astype(F32) + keep[at].astype(F32)).astype(BF16)
        copy = remote(relay.at[at], hop.at[pl.ds(rows + n * half, half)], sr.at[4 + n], rr.at[4 + n], {"head": to})
        copy.start()
        ends.append(copy)
    mine = share(row_at).astype(F32)
    for n, at in ((1, upper), (0, lower)):
        lands[n].wait_recv()
        ends[1 - n].wait_recv()
        top = 0 if n == 1 else half
        out_ref[at] = (
            mine[top : top + half] + land[at].astype(F32) + hop[pl.ds(rows + top, half)].astype(F32)
        ).astype(BF16)

    edge.wait_send()
    for copy in sends + hops + lands + ends:
        copy.wait_send()
    for d in range(1, groups):

        @pl.when(team + d < groups)
        def _():
            remote(
                total, total_got.at[team], s2.at[d], r2.at[team], {"seq": mates[d - 1]}
            ).wait_send()


def shards(
    hidden,
    w_query,
    w_key,
    w_value,
    w_gate,
    w_beta,
    conv_query,
    conv_key,
    conv_value,
    norm_gain,
    w_out,
):
    size_seq, size_head = lax.axis_size("seq"), lax.axis_size("head")
    rows, depth = hidden.shape
    wide = w_value.shape[1]
    heads = wide // DV
    groups = size_seq // heads
    tile = w_out.shape[1] // size_head
    vmem = pl.BlockSpec(memory_space=pltpu.VMEM)
    hbm = pl.BlockSpec(memory_space=pl.ANY)
    like = lambda a: pltpu.VMEM(a.shape, a.dtype)
    dma = pltpu.SemaphoreType.DMA
    bufs = [like(a) for a in (hidden, w_query, w_key, w_value, w_gate, w_out)]
    bufs += [pltpu.VMEM((HALO, depth), BF16), dma((6,)), dma, dma]
    rule = [
        pltpu.VMEM((rows + 8, wide), F32),
        pltpu.VMEM((rows, wide), F32),
        pltpu.VMEM((rows, wide), BF16),
        pltpu.VMEM((heads, DK, DK + DV), BF16),
    ]
    scan = [
        pltpu.VMEM((heads, DK, DK + DV), BF16),
        pltpu.VMEM((DK, DK + DV), BF16),
        pltpu.VMEM((groups, DK, DK + DV), BF16),
        pltpu.VMEM((heads, DK, DV), BF16),
        pltpu.VMEM((heads, DK, DV), BF16),
    ]
    scan += [dma((heads,)), dma((heads,)), dma((groups,)), dma((groups,)), dma((heads,)), dma((heads,))]
    shares = [pltpu.VMEM((rows, wide), F32), pltpu.VMEM((rows, wide), BF16)]
    shares += [pltpu.VMEM((rows, tile), BF16)] * 4
    shares += [pltpu.VMEM((2 * rows, tile), BF16), pltpu.VMEM((rows, tile), BF16), dma((6,)), dma((6,))]
    return pl.pallas_call(
        functools.partial(layer_kernel, (size_seq, size_head, heads)),
        in_specs=[hbm] * 5 + [vmem] * 5 + [hbm],
        out_specs=vmem,
        out_shape=jax.ShapeDtypeStruct((rows, tile), BF16),
        scratch_shapes=[bufs, rule, scan, shares],
        compiler_params=pltpu.CompilerParams(collective_id=0, has_side_effects=True),
        name="layer",
    )(
        hidden,
        w_query,
        w_key,
        w_value,
        w_gate,
        w_beta.T,
        conv_query,
        conv_key,
        conv_value,
        norm_gain.reshape(1, DV),
        w_out,
    )


def solution(mesh):
    in_specs = (
        P("seq", None),
        P(None, "head"),
        P(None, "head"),
        P(None, "head"),
        P(None, "head"),
        P(None, "head"),
        P(None, "head"),
        P(None, "head"),
        P(None, "head"),
        P(),
        P("head", None),
    )
    out_specs = P("seq", "head")
    return jax.shard_map(shards, mesh=mesh, in_specs=in_specs, out_specs=out_specs, check_vma=False)
```

```python
import functools

import jax
import jax.numpy as jnp
from jax import lax
from jax.experimental import pallas as pl
from jax.experimental.pallas import tpu as pltpu
from jax.sharding import PartitionSpec as P

DK = 128
DV = 128
KER = 4
HALO = 16
VALUE_PARTS = 2
eps_norm = 1e-06
F32 = jnp.float32
BF16 = jnp.bfloat16
MESH = pl.DeviceIdType.MESH


def mm(a, b):
    return jnp.dot(a, b, preferred_element_type=F32)


def mm_nt(a, b):
    return lax.dot_general(a, b, (((1,), (1,)), ((), ())), preferred_element_type=F32)


def mm_tn(a, b):
    return lax.dot_general(a, b, (((0,), (0,)), ((), ())), preferred_element_type=F32)


def sigmoid(x):
    return 0.5 + 0.5 * jnp.tanh(0.5 * x)


def silu(x):
    half = 0.5 * x
    return half + half * jnp.tanh(half)


def unit_rows(x):
    return x * lax.rsqrt(jnp.sum(x * x, axis=-1, keepdims=True) + eps_norm)


def block_solve(systems):
    n = systems[0].shape[0]
    row = lax.broadcasted_iota(jnp.int32, (n, n), 0)
    col = lax.broadcasted_iota(jnp.int32, (n, n), 1)
    zero = jnp.zeros((), BF16)

    def pick(a, size, first, stride):
        lane = lax.broadcasted_iota(jnp.int32, (size, n), 1) // size
        out = jnp.zeros((size, n), F32)
        for b in range(first, n // size, stride):
            out = jnp.where(lane == b - first, a[b * size : (b + 1) * size], out)
        return out

    def spread(x, size, mask):
        return jnp.where(mask, jnp.concatenate([x.astype(BF16)] * (n // size), axis=0), zero)

    size = 16
    same = (row // size) == (col // size)
    small = lax.broadcasted_iota(jnp.int32, (size, n), 1) % size
    eye = (small == lax.broadcasted_iota(jnp.int32, (size, n), 0)).astype(F32)
    powers = [-pick(a, size, 0, 1) for a in systems]
    solved = [eye + p for p in powers]
    powers = [mm(p.astype(BF16), spread(p, size, same)) for p in powers]
    for last in (False, False, True):
        wide = [spread(p, size, same) for p in powers]
        if last:
            solved = [x + mm(x.astype(BF16), w) for x, w in zip(solved, wide)]
        else:
            both = [
                mm(jnp.concatenate([x, p], axis=0).astype(BF16), w)
                for x, p, w in zip(solved, powers, wide)
            ]
            solved = [x + y[:size] for x, y in zip(solved, both)]
            powers = [y[size:] for y in both]
    while size < n:
        same = (row // size) == (col // size)
        below = ((row // size) == (col // size) + 1) & ((row // size) % 2 == 1)
        odd = (lax.broadcasted_iota(jnp.int32, (size, n), 1) // size) % 2 == 1
        cross = [
            mm(pick(a, size, 1, 2).astype(BF16), spread(x, size, same))
            for a, x in zip(systems, solved)
        ]
        cross = [mm(x.astype(BF16), spread(c, size, below)) for x, c in zip(solved, cross)]
        solved = [
            jnp.concatenate([jnp.where(odd, 0.0, x), jnp.where(odd, x, -c)], axis=0)
            for x, c in zip(solved, cross)
        ]
        size *= 2
    return [x.astype(BF16) for x in solved]


def key_side(queries, keys, betas):
    rows = keys[0].shape[0]
    half = rows // 2
    row = lax.broadcasted_iota(jnp.int32, (half, half), 0)
    col = lax.broadcasted_iota(jnp.int32, (half, half), 1)
    qb = [q.astype(BF16) for q in queries]
    kb = [k.astype(BF16) for k in keys]
    grams = [mm_nt(k, k) for k in kb]
    scores = [mm_nt(q, k) for q, k in zip(qb, kb)]
    systems, corners = [], []
    for gram, many in zip(grams, betas):
        first = jnp.where(row > col, gram[:half, :half], 0.0)
        last = jnp.where(row > col, gram[half:, half:], 0.0)
        for b in many:
            systems += [b[:half] * first, b[half:] * last]
            corners.append((b[half:] * gram[half:, :half]).astype(BF16))
    inverses = block_solve(systems)
    masked = []
    for score in scores:
        upper = jnp.where(row >= col, score[:half, :half], 0.0).astype(BF16)
        lower = jnp.concatenate(
            [score[half:, :half], jnp.where(row >= col, score[half:, half:], 0.0)], axis=1
        ).astype(BF16)
        masked.append((upper, lower))
    return kb, masked, list(zip(inverses[::2], inverses[1::2], corners))


def value_side(solves, keys, values, betas):
    half = keys[0].shape[0] // 2
    sides = [jnp.concatenate([b * k, b * v], axis=1) for k, v, b in zip(keys, values, betas)]
    tops = [mm(x[0], s[:half].astype(BF16)).astype(BF16) for x, s in zip(solves, sides)]
    rest = [(s[half:] - mm(x[2], t)).astype(BF16) for s, x, t in zip(sides, solves, tops)]
    ends = [mm(x[1], r).astype(BF16) for x, r in zip(solves, rest)]
    return [jnp.concatenate(pair, axis=0) for pair in zip(tops, ends)]


def join(first, second):
    return first + second - mm(second[:, :DK].astype(BF16), first.astype(BF16))


def layer_kernel(
    sizes, hid, wq, wk, wv, wg, wb, cq, ck, cv, gain, wo, out_ref, bufs, rule, scan, shares
):
    size_seq, size_head, members = sizes
    groups = size_seq // members
    me, row_at = lax.axis_index("seq"), lax.axis_index("head")
    slot, team = lax.rem(me, members), me // members
    after, before = lax.rem(me + 1, size_seq), lax.rem(me + size_seq - 1, size_seq)
    peers = [team * members + lax.rem(slot + d, members) for d in range(1, members)]
    mates = [lax.rem(team + d, groups) * members + slot for d in range(1, groups)]
    others = [lax.rem(row_at + d, size_head) for d in range(1, size_head)]

    def remote(src, dst, send, recv, to):
        return pltpu.make_async_remote_copy(
            src_ref=src, dst_ref=dst, send_sem=send, recv_sem=recv, device_id=to, device_id_type=MESH
        )

    h_buf, q_buf, k_buf, v_buf, g_buf, o_buf, halo, load_sem, edge_send, edge_recv = bufs
    rows, wide = h_buf.shape[0], v_buf.shape[1]
    part_wide = wide // VALUE_PARTS
    ways = [(hid, h_buf), (wk, k_buf), (wq, q_buf)]
    for n in range(VALUE_PARTS):
        at = pl.ds(n * part_wide, part_wide)
        ways.append((wv.at[:, at], v_buf.at[:, at]))
    ways += [(wg, g_buf), (wo, o_buf)]
    loads = [pltpu.make_async_copy(src, dst, load_sem.at[i]) for i, (src, dst) in enumerate(ways)]
    load_h, load_k, load_q, *load_v, load_g, load_o = loads
    for copy in loads[:-2]:
        copy.start()

    barrier = pltpu.get_barrier_semaphore()
    greeted = [{"seq": i} for i in [after, before] + peers + mates]
    greeted += [{"head": i} for i in (others[0], others[-1])]
    for to in greeted:
        pl.semaphore_signal(barrier, inc=1, device_id=to, device_id_type=MESH)
    pl.semaphore_wait(barrier, len(greeted))

    edge = remote(hid.at[pl.ds(rows - HALO, HALO)], halo, edge_send, edge_recv, {"seq": after})
    edge.start()

    ext_ref, ext_k, ext_q, part_ref, ask_ref, carry_ref = rule
    load_h.wait()
    h = h_buf[...]
    beta = 0.05 + 0.15 * sigmoid(mm_nt(h, wb[...]))
    lane = lax.broadcasted_iota(jnp.int32, beta.shape, 1)
    betas = [
        jnp.sum(jnp.where(lane == j, beta, 0.0), axis=1, keepdims=True)
        for j in range(beta.shape[1])
    ]
    def convolve(ext, taps, width):
        t = 0.5 * taps.astype(F32)
        summed = t[:1] * ext[pl.ds(8 - KER + 1, rows), :width]
        for j in range(1, KER):
            summed = summed + t[j : j + 1] * ext[pl.ds(8 - KER + 1 + j, rows), :width]
        x = summed + summed * jnp.tanh(summed)
        return [x[:, j * DK : (j + 1) * DK] for j in range(width // DK)]

    load_k.wait()
    ext_k[8:] = mm(h, k_buf[...])
    load_q.wait()
    ext_q[8:] = mm(h, q_buf[...])
    edge.wait_recv()
    border = halo[...]
    border = jnp.where(me > 0, border, jnp.zeros_like(border))
    tall = jnp.concatenate([border, h], axis=0)
    ext_k[:8] = mm(border, k_buf[...])[HALO - 8 :]
    ext_q[:8] = mm(border, q_buf[...])[HALO - 8 :]
    keys = [unit_rows(x) for x in convolve(ext_k, ck[...], k_buf.shape[1])]
    queries = [unit_rows(x) for x in convolve(ext_q, cq[...], q_buf.shape[1])]
    heads = len(betas)
    group = heads // len(keys)
    kb, masked, solves = key_side(
        queries, keys, [betas[j : j + group] for j in range(0, heads, group)]
    )

    got, total, total_got, start, state_ref, s1, r1, s2, r2, s3, r3 = scan

    def carry_copy(j):
        return remote(
            carry_ref.at[j], got.at[slot], s1.at[j], r1.at[slot], {"seq": team * members + j}
        )

    sides = []
    per = heads // VALUE_PARTS
    for n in range(VALUE_PARTS):
        load_v[n].wait()
        if n == VALUE_PARTS - 1:
            load_g.start()
            load_o.start()
        at = pl.ds(n * part_wide, part_wide)
        ext_ref[...] = mm(tall, v_buf[:, at])[HALO - 8 :]
        values = convolve(ext_ref, cv[:, at], part_wide)
        mine = range(n * per, (n + 1) * per)
        some = value_side(
            [solves[j] for j in mine],
            [keys[j // group] for j in mine],
            values,
            [betas[j] for j in mine],
        )
        for j, side in zip(mine, some):
            carry_ref[j] = mm_tn(kb[j // group], side).astype(BF16)

            @pl.when(slot != j)
            def _():
                carry_copy(j).start()

            @pl.when(slot == j)
            def _():
                got[j] = carry_ref[j]

        sides += some

    half = rows // 2
    for j, side in enumerate(sides):
        at = slice(j * DV, (j + 1) * DV)
        upper, lower = masked[j // group]
        seen = jnp.concatenate([mm(upper, side[:half]), mm(lower, side)], axis=0)
        part_ref[:, at] = seen[:, DK:]
        ask_ref[:, at] = (queries[j // group] - seen[:, :DK]).astype(BF16)
    gate_ref, gated_ref, keep, relay, opp, direct, hop, land, sr, rr = shares
    load_g.wait()
    gain_row = gain[...].astype(F32)
    gate = silu(mm(h, g_buf[...]).astype(BF16).astype(F32))
    for j in range(heads):
        at = slice(j * DV, (j + 1) * DV)
        gate_ref[:, at] = gate[:, at] * gain_row

    sends = []
    spans = []
    for i in range(members):

        @pl.when(slot != i)
        def _():
            remote(got.at[i], got.at[i], s1.at[0], r1.at[i], {"seq": peers[0]}).wait_recv()

        spans.append(got[i].astype(F32))
    level = {(i, i + 1): x for i, x in enumerate(spans)}
    size = 1
    while size < members:
        for i in range(0, members, 2 * size):
            level[i, i + 2 * size] = join(level[i, i + size], level[i + size, i + 2 * size])
        size *= 2
    total[...] = level[0, members].astype(BF16)
    for d in range(1, groups):

        @pl.when(team + d < groups)
        def _():
            remote(
                total, total_got.at[team], s2.at[d], r2.at[team], {"seq": mates[d - 1]}
            ).start()

    prefix = [None]
    for i in range(1, members):
        size = i & -i
        if i > size:
            level[0, i] = join(level[0, i - size], level[i - size, i])
        prefix.append(level[0, i])
    state = jnp.zeros((DK, DV), F32)
    for i in range(groups - 1):

        @pl.when(team > i)
        def _():
            remote(total_got.at[i], total_got.at[i], s2.at[0], r2.at[i], {"seq": mates[0]}).wait_recv()

        whole = total_got[i].astype(F32)
        moved = whole[:, DK:]
        if i > 0:
            moved = moved + state - mm(whole[:, :DK].astype(BF16), state.astype(BF16))
        state = jnp.where(team > i, moved, state)
    entry = state
    rounded = entry.astype(BF16)
    start[0] = rounded
    for i in range(1, members):
        begin = entry + prefix[i][:, DK:] - mm(prefix[i][:, :DK].astype(BF16), rounded)
        start[i] = begin.astype(BF16)
    turns = [(n * members // 4, c) for n in (0, 1, 3, 2) for c in range(members // 4)]
    near = [
        lax.rem(slot - lax.rem(slot, members // 4) + n, members) + lax.rem(slot + c, members // 4)
        for n, c in turns
    ]
    for d in reversed(range(1, members)):
        copy = remote(
            start.at[near[d]],
            state_ref.at[slot],
            s3.at[d],
            r3.at[slot],
            {"seq": team * members + near[d]},
        )
        copy.start()
        sends.append(copy)
    state_ref[slot] = start[slot]
    for d in range(members):
        i = near[d]
        if d > 0:
            remote(state_ref.at[i], state_ref.at[i], s3.at[0], r3.at[i], {"seq": peers[0]}).wait_recv()
        at = pl.ds(pl.multiple_of(i * DV, DV), DV)
        attended = part_ref[:, at] + mm(ask_ref[:, at], state_ref[i])
        scale = lax.rsqrt(jnp.mean(attended * attended, axis=-1, keepdims=True) + eps_norm)
        gated_ref[:, at] = (attended * scale * gate_ref[:, at]).astype(BF16)

    load_o.wait()
    gated = gated_ref[...]
    tile = out_ref.shape[1]
    half = rows // 2
    upper, lower = pl.ds(0, half), pl.ds(half, half)

    def share(to):
        columns = pl.ds(pl.multiple_of(to * tile, tile), tile)
        return mm(gated, o_buf[:, columns]).astype(BF16)

    right, far, left = others
    opp[...] = share(far)
    hops = [
        remote(opp.at[upper], hop.at[upper], sr.at[0], rr.at[0], {"head": right}),
        remote(opp.at[lower], hop.at[lower], sr.at[1], rr.at[1], {"head": left}),
    ]
    for copy in hops:
        copy.start()
    to_right, to_left = share(right), share(left)
    keep[upper], keep[lower] = to_right[:half], to_left[half:]
    direct[lower], direct[upper] = to_right[half:], to_left[:half]
    lands = [
        remote(direct.at[lower], land.at[lower], sr.at[2], rr.at[2], {"head": right}),
        remote(direct.at[upper], land.at[upper], sr.at[3], rr.at[3], {"head": left}),
    ]
    for copy in lands:
        copy.start()
    ends = []
    for n, (at, to) in enumerate(((upper, right), (lower, left))):
        hops[n].wait_recv()
        relay[at] = (hop[at].astype(F32) + keep[at].astype(F32)).astype(BF16)
        copy = remote(relay.at[at], hop.at[pl.ds(rows + n * half, half)], sr.at[4 + n], rr.at[4 + n], {"head": to})
        copy.start()
        ends.append(copy)
    mine = share(row_at).astype(F32)
    for n, at in ((1, upper), (0, lower)):
        lands[n].wait_recv()
        ends[1 - n].wait_recv()
        top = 0 if n == 1 else half
        out_ref[at] = (
            mine[top : top + half] + land[at].astype(F32) + hop[pl.ds(rows + top, half)].astype(F32)
        ).astype(BF16)

    edge.wait_send()
    for j in range(members):

        @pl.when(slot != j)
        def _():
            carry_copy(j).wait_send()

    for copy in sends + hops + lands + ends:
        copy.wait_send()
    for d in range(1, groups):

        @pl.when(team + d < groups)
        def _():
            remote(
                total, total_got.at[team], s2.at[d], r2.at[team], {"seq": mates[d - 1]}
            ).wait_send()


def shards(
    hidden,
    w_query,
    w_key,
    w_value,
    w_gate,
    w_beta,
    conv_query,
    conv_key,
    conv_value,
    norm_gain,
    w_out,
):
    size_seq, size_head = lax.axis_size("seq"), lax.axis_size("head")
    rows, depth = hidden.shape
    wide = w_value.shape[1]
    heads = wide // DV
    groups = size_seq // heads
    tile = w_out.shape[1] // size_head
    vmem = pl.BlockSpec(memory_space=pltpu.VMEM)
    hbm = pl.BlockSpec(memory_space=pl.ANY)
    like = lambda a: pltpu.VMEM(a.shape, a.dtype)
    dma = pltpu.SemaphoreType.DMA
    bufs = [like(a) for a in (hidden, w_query, w_key, w_value, w_gate, w_out)]
    bufs += [pltpu.VMEM((HALO, depth), BF16), dma((5 + VALUE_PARTS,)), dma, dma]
    rule = [
        pltpu.VMEM((rows + 8, wide // VALUE_PARTS), F32),
        pltpu.VMEM((rows + 8, w_key.shape[1]), F32),
        pltpu.VMEM((rows + 8, w_query.shape[1]), F32),
        pltpu.VMEM((rows, wide), F32),
        pltpu.VMEM((rows, wide), BF16),
        pltpu.VMEM((heads, DK, DK + DV), BF16),
    ]
    scan = [
        pltpu.VMEM((heads, DK, DK + DV), BF16),
        pltpu.VMEM((DK, DK + DV), BF16),
        pltpu.VMEM((groups, DK, DK + DV), BF16),
        pltpu.VMEM((heads, DK, DV), BF16),
        pltpu.VMEM((heads, DK, DV), BF16),
    ]
    scan += [dma((heads,)), dma((heads,)), dma((groups,)), dma((groups,)), dma((heads,)), dma((heads,))]
    shares = [pltpu.VMEM((rows, wide), F32), pltpu.VMEM((rows, wide), BF16)]
    shares += [pltpu.VMEM((rows, tile), BF16)] * 4
    shares += [pltpu.VMEM((2 * rows, tile), BF16), pltpu.VMEM((rows, tile), BF16), dma((6,)), dma((6,))]
    return pl.pallas_call(
        functools.partial(layer_kernel, (size_seq, size_head, heads)),
        in_specs=[hbm] * 5 + [vmem] * 5 + [hbm],
        out_specs=vmem,
        out_shape=jax.ShapeDtypeStruct((rows, tile), BF16),
        scratch_shapes=[bufs, rule, scan, shares],
        compiler_params=pltpu.CompilerParams(collective_id=0, has_side_effects=True),
        name="layer",
    )(
        hidden,
        w_query,
        w_key,
        w_value,
        w_gate,
        w_beta.T,
        conv_query,
        conv_key,
        conv_value,
        norm_gain.reshape(1, DV),
        w_out,
    )


def solution(mesh):
    in_specs = (
        P("seq", None),
        P(None, "head"),
        P(None, "head"),
        P(None, "head"),
        P(None, "head"),
        P(None, "head"),
        P(None, "head"),
        P(None, "head"),
        P(None, "head"),
        P(),
        P("head", None),
    )
    out_specs = P("seq", "head")
    return jax.shard_map(shards, mesh=mesh, in_specs=in_specs, out_specs=out_specs, check_vma=False)
```

```python
import functools

import jax
import jax.numpy as jnp
from jax import lax
from jax.experimental import pallas as pl
from jax.experimental.pallas import tpu as pltpu
from jax.sharding import PartitionSpec as P

DK = 128
DV = 128
KER = 4
HALO = 16
eps_norm = 1e-06
F32 = jnp.float32
BF16 = jnp.bfloat16
MESH = pl.DeviceIdType.MESH


def mm(a, b):
    return jnp.dot(a, b, preferred_element_type=F32)


def mm_nt(a, b):
    return lax.dot_general(a, b, (((1,), (1,)), ((), ())), preferred_element_type=F32)


def mm_tn(a, b):
    return lax.dot_general(a, b, (((0,), (0,)), ((), ())), preferred_element_type=F32)


def sigmoid(x):
    return 0.5 + 0.5 * jnp.tanh(0.5 * x)


def silu(x):
    half = 0.5 * x
    return half + half * jnp.tanh(half)


def unit_rows(x):
    return x * lax.rsqrt(jnp.sum(x * x, axis=-1, keepdims=True) + eps_norm)


def block_solve(systems, fill):
    n = systems[0].shape[0]
    row = lax.broadcasted_iota(jnp.int32, (n, n), 0)
    col = lax.broadcasted_iota(jnp.int32, (n, n), 1)
    zero = jnp.zeros((), BF16)

    def pick(a, size, first, stride):
        lane = lax.broadcasted_iota(jnp.int32, (size, n), 1) // size
        out = jnp.zeros((size, n), F32)
        for b in range(first, n // size, stride):
            out = jnp.where(lane == b - first, a[b * size : (b + 1) * size], out)
        return out

    def spread(x, size, mask):
        return jnp.where(mask, jnp.concatenate([x.astype(BF16)] * (n // size), axis=0), zero)

    size = 16
    same = (row // size) == (col // size)
    small = lax.broadcasted_iota(jnp.int32, (size, n), 1) % size
    eye = (small == lax.broadcasted_iota(jnp.int32, (size, n), 0)).astype(F32)
    powers = [-pick(a, size, 0, 1) for a in systems]
    solved = [eye + p for p in powers]
    powers = [mm(p.astype(BF16), spread(p, size, same)) for p in powers]
    fill()
    for last in (False, False, True):
        wide = [spread(p, size, same) for p in powers]
        if last:
            solved = [x + mm(x.astype(BF16), w) for x, w in zip(solved, wide)]
        else:
            both = [
                mm(jnp.concatenate([x, p], axis=0).astype(BF16), w)
                for x, p, w in zip(solved, powers, wide)
            ]
            solved = [x + y[:size] for x, y in zip(solved, both)]
            powers = [y[size:] for y in both]
        fill()
    while size < n:
        same = (row // size) == (col // size)
        below = ((row // size) == (col // size) + 1) & ((row // size) % 2 == 1)
        odd = (lax.broadcasted_iota(jnp.int32, (size, n), 1) // size) % 2 == 1
        cross = [
            mm(pick(a, size, 1, 2).astype(BF16), spread(x, size, same))
            for a, x in zip(systems, solved)
        ]
        fill()
        cross = [mm(x.astype(BF16), spread(c, size, below)) for x, c in zip(solved, cross)]
        solved = [
            jnp.concatenate([jnp.where(odd, 0.0, x), jnp.where(odd, x, -c)], axis=0)
            for x, c in zip(solved, cross)
        ]
        size *= 2
        fill()
    return [x.astype(BF16) for x in solved]


def key_side(keys, betas, fill):
    half = keys[0].shape[0] // 2
    row = lax.broadcasted_iota(jnp.int32, (half, half), 0)
    col = lax.broadcasted_iota(jnp.int32, (half, half), 1)
    kb = [k.astype(BF16) for k in keys]
    grams = [mm_nt(k, k) for k in kb]
    systems, corners = [], []
    for gram, many in zip(grams, betas):
        first = jnp.where(row > col, gram[:half, :half], 0.0)
        last = jnp.where(row > col, gram[half:, half:], 0.0)
        for b in many:
            systems += [b[:half] * first, b[half:] * last]
            corners.append((b[half:] * gram[half:, :half]).astype(BF16))
    inverses = block_solve(systems, fill)
    return kb, list(zip(inverses[::2], inverses[1::2], corners))


def query_side(queries, kb):
    half = queries[0].shape[0] // 2
    row = lax.broadcasted_iota(jnp.int32, (half, half), 0)
    col = lax.broadcasted_iota(jnp.int32, (half, half), 1)
    masked = []
    for q, k in zip(queries, kb):
        score = mm_nt(q.astype(BF16), k)
        upper = jnp.where(row >= col, score[:half, :half], 0.0).astype(BF16)
        lower = jnp.concatenate(
            [score[half:, :half], jnp.where(row >= col, score[half:, half:], 0.0)], axis=1
        ).astype(BF16)
        masked.append((upper, lower))
    return masked


def value_side(solves, sides):
    half = sides[0].shape[0] // 2
    tops = [mm(x[0], s[:half].astype(BF16)).astype(BF16) for x, s in zip(solves, sides)]
    rest = [(s[half:] - mm(x[2], t)).astype(BF16) for s, x, t in zip(sides, solves, tops)]
    ends = [mm(x[1], r).astype(BF16) for x, r in zip(solves, rest)]
    return [jnp.concatenate(pair, axis=0) for pair in zip(tops, ends)]


def join(first, second):
    return first + second - mm(second[:, :DK].astype(BF16), first.astype(BF16))


def layer_kernel(
    sizes, hid, wq, wk, wv, wg, wb, cq, ck, cv, gain, wo, out_ref, bufs, rule, scan, shares
):
    size_seq, size_head, members = sizes
    groups = size_seq // members
    me, row_at = lax.axis_index("seq"), lax.axis_index("head")
    slot, team = lax.rem(me, members), me // members
    after, before = lax.rem(me + 1, size_seq), lax.rem(me + size_seq - 1, size_seq)
    peers = [team * members + lax.rem(slot + d, members) for d in range(1, members)]
    mates = [lax.rem(team + d, groups) * members + slot for d in range(1, groups)]
    others = [lax.rem(row_at + d, size_head) for d in range(1, size_head)]

    def remote(src, dst, send, recv, to):
        return pltpu.make_async_remote_copy(
            src_ref=src, dst_ref=dst, send_sem=send, recv_sem=recv, device_id=to, device_id_type=MESH
        )

    h_buf, q_buf, k_buf, v_buf, g_buf, o_buf, halo, load_sem, edge_send, edge_recv = bufs
    rows = h_buf.shape[0]
    ways = ((hid, h_buf), (wk, k_buf), (wq, q_buf), (wv, v_buf), (wg, g_buf), (wo, o_buf))
    loads = [pltpu.make_async_copy(src, dst, load_sem.at[i]) for i, (src, dst) in enumerate(ways)]
    load_h, load_k, load_q, load_v, load_g, load_o = loads
    for copy in loads[:-2]:
        copy.start()

    barrier = pltpu.get_barrier_semaphore()
    greeted = [{"seq": i} for i in [after, before] + peers + mates]
    greeted += [{"head": i} for i in (others[0], others[-1])]
    for to in greeted:
        pl.semaphore_signal(barrier, inc=1, device_id=to, device_id_type=MESH)
    pl.semaphore_wait(barrier, len(greeted))

    edge = remote(hid.at[pl.ds(rows - HALO, HALO)], halo, edge_send, edge_recv, {"seq": after})
    edge.start()

    ext_v, ext_k, ext_q, part_ref, ask_ref, carry_ref = rule
    load_h.wait()
    h = h_buf[...]
    beta = 0.05 + 0.15 * sigmoid(mm_nt(h, wb[...]))
    lane = lax.broadcasted_iota(jnp.int32, beta.shape, 1)
    betas = [
        jnp.sum(jnp.where(lane == j, beta, 0.0), axis=1, keepdims=True)
        for j in range(beta.shape[1])
    ]
    def convolve(ext, taps, j):
        at = slice(j * DK, (j + 1) * DK)
        t = 0.5 * taps[:, at].astype(F32)
        x = ext[:, at]
        summed = t[KER - 1 :] * x
        for n in range(KER - 1):
            summed = summed + t[n : n + 1] * pltpu.roll(x, KER - 1 - n, 0)
        summed = summed[8:]
        return summed + summed * jnp.tanh(summed)

    projections = ((load_k, k_buf, ext_k), (load_q, q_buf, ext_q), (load_v, v_buf, ext_v))
    for load, w, ext in projections:
        load.wait()
        ext[8:] = mm(h, w[...])
    load_g.start()
    load_o.start()
    edge.wait_recv()
    border = halo[...]
    border = jnp.where(me > 0, border, jnp.zeros_like(border))
    for _, w, ext in projections:
        ext[:8] = mm(border, w[...])[HALO - 8 :]
    heads = len(betas)
    count = k_buf.shape[1] // DK
    group = heads // count
    keys = [unit_rows(convolve(ext_k, ck, j)) for j in range(count)]
    sides = []

    def fill():
        j = len(sides)
        if j < heads:
            b = betas[j]
            v = convolve(ext_v, cv, j)
            sides.append(jnp.concatenate([b * keys[j // group], b * v], axis=1))

    kb, solves = key_side(keys, [betas[j : j + group] for j in range(0, heads, group)], fill)
    while len(sides) < heads:
        fill()

    got, total, total_got, start, state_ref, s1, r1, s2, r2, s3, r3 = scan

    def carry_copy(j):
        return remote(
            carry_ref.at[j], got.at[slot], s1.at[j], r1.at[slot], {"seq": team * members + j}
        )

    sides = value_side(solves, sides)
    for j, side in enumerate(sides):
        carry_ref[j] = mm_tn(kb[j // group], side).astype(BF16)
    for j in range(heads):

        @pl.when(slot != j)
        def _():
            carry_copy(j).start()

    got[slot] = carry_ref[slot]

    half = rows // 2
    queries = [unit_rows(convolve(ext_q, cq, j)) for j in range(count)]
    masked = query_side(queries, kb)
    for j, side in enumerate(sides):
        at = slice(j * DV, (j + 1) * DV)
        upper, lower = masked[j // group]
        seen = jnp.concatenate([mm(upper, side[:half]), mm(lower, side)], axis=0)
        part_ref[:, at] = seen[:, DK:]
        ask_ref[:, at] = (queries[j // group] - seen[:, :DK]).astype(BF16)
    gate_ref, gated_ref, keep, relay, opp, direct, hop, land, sr, rr = shares
    load_g.wait()
    gain_row = gain[...].astype(F32)
    gate = silu(mm(h, g_buf[...]).astype(BF16).astype(F32))
    for j in range(heads):
        at = slice(j * DV, (j + 1) * DV)
        gate_ref[:, at] = gate[:, at] * gain_row

    sends = []
    spans = []
    for i in range(members):

        @pl.when(slot != i)
        def _():
            remote(got.at[i], got.at[i], s1.at[0], r1.at[i], {"seq": peers[0]}).wait_recv()

        spans.append(got[i].astype(F32))
    level = {(i, i + 1): x for i, x in enumerate(spans)}
    size = 1
    while size < members:
        for i in range(0, members, 2 * size):
            level[i, i + 2 * size] = join(level[i, i + size], level[i + size, i + 2 * size])
        size *= 2
    total[...] = level[0, members].astype(BF16)
    for d in range(1, groups):

        @pl.when(team + d < groups)
        def _():
            remote(
                total, total_got.at[team], s2.at[d], r2.at[team], {"seq": mates[d - 1]}
            ).start()

    prefix = [None]
    for i in range(1, members):
        size = i & -i
        if i > size:
            level[0, i] = join(level[0, i - size], level[i - size, i])
        prefix.append(level[0, i])
    state = jnp.zeros((DK, DV), F32)
    for i in range(groups - 1):

        @pl.when(team > i)
        def _():
            remote(total_got.at[i], total_got.at[i], s2.at[0], r2.at[i], {"seq": mates[0]}).wait_recv()

        whole = total_got[i].astype(F32)
        moved = whole[:, DK:]
        if i > 0:
            moved = moved + state - mm(whole[:, :DK].astype(BF16), state.astype(BF16))
        state = jnp.where(team > i, moved, state)
    entry = state
    rounded = entry.astype(BF16)
    start[0] = rounded
    for i in range(1, members):
        begin = entry + prefix[i][:, DK:] - mm(prefix[i][:, :DK].astype(BF16), rounded)
        start[i] = begin.astype(BF16)
    turns = [(n * members // 4, c) for n in (0, 1, 3, 2) for c in range(members // 4)]
    near = [
        lax.rem(slot - lax.rem(slot, members // 4) + n, members) + lax.rem(slot + c, members // 4)
        for n, c in turns
    ]
    for d in reversed(range(1, members)):
        copy = remote(
            start.at[near[d]],
            state_ref.at[slot],
            s3.at[d],
            r3.at[slot],
            {"seq": team * members + near[d]},
        )
        copy.start()
        sends.append(copy)
    state_ref[slot] = start[slot]
    for d in range(0, members, 2):
        for i in near[max(d, 1) : d + 2]:
            remote(state_ref.at[i], state_ref.at[i], s3.at[0], r3.at[i], {"seq": peers[0]}).wait_recv()
        at = [pl.ds(pl.multiple_of(i * DV, DV), DV) for i in near[d : d + 2]]
        pair = [part_ref[:, c] + mm(ask_ref[:, c], state_ref[i]) for c, i in zip(at, near[d : d + 2])]
        scales = [lax.rsqrt(jnp.mean(x * x, axis=-1, keepdims=True) + eps_norm) for x in pair]
        for c, x, scale in zip(at, pair, scales):
            gated_ref[:, c] = (x * scale * gate_ref[:, c]).astype(BF16)

    load_o.wait()
    gated = gated_ref[...]
    tile = out_ref.shape[1]
    half = rows // 2
    upper, lower = pl.ds(0, half), pl.ds(half, half)

    def share(to):
        columns = pl.ds(pl.multiple_of(to * tile, tile), tile)
        return mm(gated, o_buf[:, columns]).astype(BF16)

    right, far, left = others
    opp[...] = share(far)
    hops = [
        remote(opp.at[upper], hop.at[upper], sr.at[0], rr.at[0], {"head": right}),
        remote(opp.at[lower], hop.at[lower], sr.at[1], rr.at[1], {"head": left}),
    ]
    for copy in hops:
        copy.start()
    to_right, to_left = share(right), share(left)
    keep[upper], keep[lower] = to_right[:half], to_left[half:]
    direct[lower], direct[upper] = to_right[half:], to_left[:half]
    lands = [
        remote(direct.at[lower], land.at[lower], sr.at[2], rr.at[2], {"head": right}),
        remote(direct.at[upper], land.at[upper], sr.at[3], rr.at[3], {"head": left}),
    ]
    for copy in lands:
        copy.start()
    ends = []
    for n, (at, to) in enumerate(((upper, right), (lower, left))):
        hops[n].wait_recv()
        relay[at] = (hop[at].astype(F32) + keep[at].astype(F32)).astype(BF16)
        copy = remote(relay.at[at], hop.at[pl.ds(rows + n * half, half)], sr.at[4 + n], rr.at[4 + n], {"head": to})
        copy.start()
        ends.append(copy)
    mine = share(row_at).astype(F32)
    for n, at in ((1, upper), (0, lower)):
        lands[n].wait_recv()
        ends[1 - n].wait_recv()
        top = 0 if n == 1 else half
        out_ref[at] = (
            mine[top : top + half] + land[at].astype(F32) + hop[pl.ds(rows + top, half)].astype(F32)
        ).astype(BF16)

    edge.wait_send()
    for j in range(members):

        @pl.when(slot != j)
        def _():
            carry_copy(j).wait_send()

    for copy in sends + hops + lands + ends:
        copy.wait_send()
    for d in range(1, groups):

        @pl.when(team + d < groups)
        def _():
            remote(
                total, total_got.at[team], s2.at[d], r2.at[team], {"seq": mates[d - 1]}
            ).wait_send()


def shards(
    hidden,
    w_query,
    w_key,
    w_value,
    w_gate,
    w_beta,
    conv_query,
    conv_key,
    conv_value,
    norm_gain,
    w_out,
):
    size_seq, size_head = lax.axis_size("seq"), lax.axis_size("head")
    rows, depth = hidden.shape
    wide = w_value.shape[1]
    heads = wide // DV
    groups = size_seq // heads
    tile = w_out.shape[1] // size_head
    vmem = pl.BlockSpec(memory_space=pltpu.VMEM)
    hbm = pl.BlockSpec(memory_space=pl.ANY)
    like = lambda a: pltpu.VMEM(a.shape, a.dtype)
    dma = pltpu.SemaphoreType.DMA
    bufs = [like(a) for a in (hidden, w_query, w_key, w_value, w_gate, w_out)]
    bufs += [pltpu.VMEM((HALO, depth), BF16), dma((6,)), dma, dma]
    rule = [
        pltpu.VMEM((rows + 8, wide), F32),
        pltpu.VMEM((rows + 8, w_key.shape[1]), F32),
        pltpu.VMEM((rows + 8, w_query.shape[1]), F32),
        pltpu.VMEM((rows, wide), F32),
        pltpu.VMEM((rows, wide), BF16),
        pltpu.VMEM((heads, DK, DK + DV), BF16),
    ]
    scan = [
        pltpu.VMEM((heads, DK, DK + DV), BF16),
        pltpu.VMEM((DK, DK + DV), BF16),
        pltpu.VMEM((groups, DK, DK + DV), BF16),
        pltpu.VMEM((heads, DK, DV), BF16),
        pltpu.VMEM((heads, DK, DV), BF16),
    ]
    scan += [dma((heads,)), dma((heads,)), dma((groups,)), dma((groups,)), dma((heads,)), dma((heads,))]
    shares = [pltpu.VMEM((rows, wide), F32), pltpu.VMEM((rows, wide), BF16)]
    shares += [pltpu.VMEM((rows, tile), BF16)] * 4
    shares += [pltpu.VMEM((2 * rows, tile), BF16), pltpu.VMEM((rows, tile), BF16), dma((6,)), dma((6,))]
    return pl.pallas_call(
        functools.partial(layer_kernel, (size_seq, size_head, heads)),
        in_specs=[hbm] * 5 + [vmem] * 5 + [hbm],
        out_specs=vmem,
        out_shape=pltpu.VMEM((rows, tile), BF16),
        scratch_shapes=[bufs, rule, scan, shares],
        compiler_params=pltpu.CompilerParams(collective_id=0, has_side_effects=True),
        name="layer",
    )(
        hidden,
        w_query,
        w_key,
        w_value,
        w_gate,
        w_beta.T,
        conv_query,
        conv_key,
        conv_value,
        norm_gain.reshape(1, DV),
        w_out,
    )


def solution(mesh):
    in_specs = (
        P("seq", None),
        P(None, "head"),
        P(None, "head"),
        P(None, "head"),
        P(None, "head"),
        P(None, "head"),
        P(None, "head"),
        P(None, "head"),
        P(None, "head"),
        P(),
        P("head", None),
    )
    out_specs = P("seq", "head")
    return jax.shard_map(shards, mesh=mesh, in_specs=in_specs, out_specs=out_specs, check_vma=False)
```

```python
import functools

import jax
import jax.numpy as jnp
from jax import lax
from jax.experimental import pallas as pl
from jax.experimental.pallas import tpu as pltpu
from jax.sharding import PartitionSpec as P

DK = 128
DV = 128
KER = 4
HALO = 16
FILL = 2
eps_norm = 1e-06
F32 = jnp.float32
BF16 = jnp.bfloat16
MESH = pl.DeviceIdType.MESH


def mm(a, b):
    return jnp.dot(a, b, preferred_element_type=F32)


def mm_nt(a, b):
    return lax.dot_general(a, b, (((1,), (1,)), ((), ())), preferred_element_type=F32)


def mm_tn(a, b):
    return lax.dot_general(a, b, (((0,), (0,)), ((), ())), preferred_element_type=F32)


def sigmoid(x):
    return 0.5 + 0.5 * jnp.tanh(0.5 * x)


def silu(x):
    half = 0.5 * x
    return half + half * jnp.tanh(half)


def unit_rows(x):
    return x * lax.rsqrt(jnp.sum(x * x, axis=-1, keepdims=True) + eps_norm)


def block_solve(sys_ref, x_ref, fill):
    count, n = sys_ref.shape[:2]
    zero = jnp.zeros((), BF16)

    def indices():
        return (
            lax.broadcasted_iota(jnp.int32, (n, n), 0),
            lax.broadcasted_iota(jnp.int32, (n, n), 1),
        )

    def pick(i, size, first, stride):
        lane = lax.broadcasted_iota(jnp.int32, (size, n), 1) // size
        out = jnp.zeros((size, n), F32)
        for b in range(first, n // size, stride):
            out = jnp.where(lane == b - first, sys_ref[i, b * size : (b + 1) * size], out)
        return out

    def spread(x, size, mask):
        return jnp.where(mask, jnp.concatenate([x.astype(BF16)] * (n // size), axis=0), zero)

    def series():
        size = 16
        row, col = indices()
        same = (row // size) == (col // size)
        small = lax.broadcasted_iota(jnp.int32, (size, n), 1) % size
        eye = (small == lax.broadcasted_iota(jnp.int32, (size, n), 0)).astype(F32)
        powers = [-pick(i, size, 0, 1) for i in range(count)]
        solved = [eye + p for p in powers]
        powers = [mm(p.astype(BF16), spread(p, size, same)) for p in powers]
        for last in (False, False, True):
            wide = [spread(p, size, same) for p in powers]
            if last:
                solved = [x + mm(x.astype(BF16), w) for x, w in zip(solved, wide)]
            else:
                both = [
                    mm(jnp.concatenate([x, p], axis=0).astype(BF16), w)
                    for x, p, w in zip(solved, powers, wide)
                ]
                solved = [x + y[:size] for x, y in zip(solved, both)]
                powers = [y[size:] for y in both]
        for i in range(count):
            x_ref[i, :size] = solved[i]
        fill()

    series()
    size = 16
    while size < n:

        def double(size):
            row, col = indices()
            same = (row // size) == (col // size)
            below = ((row // size) == (col // size) + 1) & ((row // size) % 2 == 1)
            odd = (lax.broadcasted_iota(jnp.int32, (size, n), 1) // size) % 2 == 1
            solved = [x_ref[i, :size] for i in range(count)]
            cross = [
                mm(pick(i, size, 1, 2).astype(BF16), spread(x, size, same))
                for i, x in enumerate(solved)
            ]
            cross = [mm(x.astype(BF16), spread(c, size, below)) for x, c in zip(solved, cross)]
            for i in range(count):
                x_ref[i, :size] = jnp.where(odd, 0.0, solved[i])
                x_ref[i, size : 2 * size] = jnp.where(odd, solved[i], -cross[i])
            fill()

        double(size)
        size *= 2


def query_side(queries, kb):
    half = queries[0].shape[0] // 2
    row = lax.broadcasted_iota(jnp.int32, (half, half), 0)
    col = lax.broadcasted_iota(jnp.int32, (half, half), 1)
    masked = []
    for q, k in zip(queries, kb):
        score = mm_nt(q.astype(BF16), k)
        upper = jnp.where(row >= col, score[:half, :half], 0.0).astype(BF16)
        lower = jnp.concatenate(
            [score[half:, :half], jnp.where(row >= col, score[half:, half:], 0.0)], axis=1
        ).astype(BF16)
        masked.append((upper, lower))
    return masked


def value_side(solves, sides):
    half = sides[0].shape[0] // 2
    tops = [mm(x[0], s[:half].astype(BF16)).astype(BF16) for x, s in zip(solves, sides)]
    rest = [(s[half:] - mm(x[2], t)).astype(BF16) for s, x, t in zip(sides, solves, tops)]
    ends = [mm(x[1], r).astype(BF16) for x, r in zip(solves, rest)]
    return [jnp.concatenate(pair, axis=0) for pair in zip(tops, ends)]


def join(first, second):
    return first + second - mm(second[:, :DK].astype(BF16), first.astype(BF16))


def layer_kernel(
    sizes, hid, wq, wk, wv, wg, wb, cq, ck, cv, gain, wo, out_ref, bufs, rule, scan, shares
):
    size_seq, size_head, members = sizes
    groups = size_seq // members
    me, row_at = lax.axis_index("seq"), lax.axis_index("head")
    slot, team = lax.rem(me, members), me // members
    after, before = lax.rem(me + 1, size_seq), lax.rem(me + size_seq - 1, size_seq)
    peers = [team * members + lax.rem(slot + d, members) for d in range(1, members)]
    mates = [lax.rem(team + d, groups) * members + slot for d in range(1, groups)]
    others = [lax.rem(row_at + d, size_head) for d in range(1, size_head)]

    def remote(src, dst, send, recv, to):
        return pltpu.make_async_remote_copy(
            src_ref=src, dst_ref=dst, send_sem=send, recv_sem=recv, device_id=to, device_id_type=MESH
        )

    barrier = pltpu.get_barrier_semaphore()
    greeted = [{"seq": i} for i in [after, before] + peers + mates]
    greeted += [{"head": i} for i in (others[0], others[-1])]
    for to in greeted:
        pl.semaphore_signal(barrier, inc=1, device_id=to, device_id_type=MESH)

    h_buf, q_buf, k_buf, v_buf, g_buf, o_buf, halo, load_sem, edge_send, edge_recv = bufs
    rows = h_buf.shape[0]
    ways = ((hid, h_buf), (wk, k_buf), (wq, q_buf), (wv, v_buf), (wg, g_buf), (wo, o_buf))
    loads = [pltpu.make_async_copy(src, dst, load_sem.at[i]) for i, (src, dst) in enumerate(ways)]
    load_h, load_k, load_q, load_v, load_g, load_o = loads
    for copy in loads[:-2]:
        copy.start()

    pl.semaphore_wait(barrier, len(greeted))

    edge = remote(hid.at[pl.ds(rows - HALO, HALO)], halo, edge_send, edge_recv, {"seq": after})
    edge.start()

    ext_v, ext_k, ext_q, part_ref, ask_ref, carry_ref = rule[:6]
    sys_ref, x_ref, key_ref, beta_ref, corner_ref, side_ref = rule[6:]
    load_h.wait()
    h = h_buf[...]
    beta = 0.05 + 0.15 * sigmoid(mm_nt(h, wb[...]))
    heads = beta.shape[1]
    lane = lax.broadcasted_iota(jnp.int32, (heads, heads * DK), 1) // DK
    ones = (lane == lax.broadcasted_iota(jnp.int32, (heads, heads * DK), 0)).astype(F32).astype(BF16)
    top = beta.astype(BF16)
    beta_ref[...] = mm(top, ones) + mm((beta - top.astype(F32)).astype(BF16), ones)

    def taps_over(x, t):
        summed = t[KER - 1 :] * x
        for n in range(KER - 1):
            summed = summed + t[n : n + 1] * pltpu.roll(x, KER - 1 - n, 0)
        return summed

    def convolve(ext, edge_rows, taps, j):
        at = slice(j * DK, (j + 1) * DK)
        t = 0.5 * taps[:, at].astype(F32)
        body = taps_over(ext[:, at], t)
        brink = jnp.concatenate([edge_rows[:, at], ext[:8, at]], axis=0)
        summed = jnp.concatenate([taps_over(brink, t)[8:], body[8:]], axis=0)
        return summed + summed * jnp.tanh(summed)

    projections = ((load_k, k_buf, ext_k), (load_q, q_buf, ext_q), (load_v, v_buf, ext_v))
    for load, w, ext in projections:
        load.wait()
        ext[...] = mm(h, w[...])
    load_g.start()
    load_o.start()
    edge.wait_recv()
    border = halo[...]
    border = jnp.where(me > 0, border, jnp.zeros_like(border))
    edge_k, edge_q, edge_v = [mm(border, w[...])[HALO - 8 :] for _, w, _ in projections]
    count = k_buf.shape[1] // DK
    group = heads // count
    half = rows // 2
    keys = [unit_rows(convolve(ext_k, edge_k, ck, j)) for j in range(count)]
    kb = [k.astype(BF16) for k in keys]
    row = lax.broadcasted_iota(jnp.int32, (half, half), 0)
    col = lax.broadcasted_iota(jnp.int32, (half, half), 1)
    for n, k in enumerate(kb):
        gram = mm_nt(k, k)
        first = jnp.where(row > col, gram[:half, :half], 0.0)
        last = jnp.where(row > col, gram[half:, half:], 0.0)
        key_ref[n] = keys[n]
        for j in range(n * group, (n + 1) * group):
            b = beta_ref[:, j * DK : (j + 1) * DK]
            sys_ref[2 * j] = b[:half] * first
            sys_ref[2 * j + 1] = b[half:] * last
            corner_ref[j] = (b[half:] * gram[half:, :half]).astype(BF16)
    done = []

    def fill():
        for j in range(len(done), min(len(done) + FILL, heads)):
            b = beta_ref[:, j * DK : (j + 1) * DK]
            side_ref[j, :, :DK] = b * key_ref[j // group]
            side_ref[j, :, DK:] = b * convolve(ext_v, edge_v, cv, j)
            done.append(j)

    block_solve(sys_ref, x_ref, fill)
    while len(done) < heads:
        fill()
    solves = [
        (x_ref[2 * j].astype(BF16), x_ref[2 * j + 1].astype(BF16), corner_ref[j])
        for j in range(heads)
    ]
    sides = [side_ref[j] for j in range(heads)]

    got, total, total_got, start, state_ref, s1, r1, s2, r2, s3, r3 = scan

    turns = [(n * members // 4, c) for n in (0, 1, 3, 2) for c in range(members // 4)]
    near = [
        lax.rem(slot - lax.rem(slot, members // 4) + n, members) + lax.rem(slot + c, members // 4)
        for n, c in turns
    ]

    def to_member(src, dst, send, recv, d):
        return remote(
            src.at[near[d]], dst.at[slot], send.at[d], recv.at[slot], {"seq": team * members + near[d]}
        )

    sends = []
    sides = value_side(solves, sides)
    for j, side in enumerate(sides):
        carry_ref[j] = mm_tn(kb[j // group], side).astype(BF16)
    for d in reversed(range(1, members)):
        copy = to_member(carry_ref, got, s1, r1, d)
        copy.start()
        sends.append(copy)
    got[slot] = carry_ref[slot]

    queries = [unit_rows(convolve(ext_q, edge_q, cq, j)) for j in range(count)]
    masked = query_side(queries, kb)
    for j, side in enumerate(sides):
        at = slice(j * DV, (j + 1) * DV)
        upper, lower = masked[j // group]
        seen = jnp.concatenate([mm(upper, side[:half]), mm(lower, side)], axis=0)
        part_ref[:, at] = seen[:, DK:]
        ask_ref[:, at] = (queries[j // group] - seen[:, :DK]).astype(BF16)
    gate_ref, gated_ref, keep, relay, opp, direct, hop, land, sr, rr = shares
    load_g.wait()
    gain_row = gain[...].astype(F32)
    gate = silu(mm(h, g_buf[...]).astype(BF16).astype(F32))
    for j in range(heads):
        at = slice(j * DV, (j + 1) * DV)
        gate_ref[:, at] = gate[:, at] * gain_row

    spans = []
    for i in range(members):

        @pl.when(slot != i)
        def _():
            remote(got.at[i], got.at[i], s1.at[0], r1.at[i], {"seq": peers[0]}).wait_recv()

        spans.append(got[i].astype(F32))
    level = {(i, i + 1): x for i, x in enumerate(spans)}
    size = 1
    while size < members:
        for i in range(0, members, 2 * size):
            level[i, i + 2 * size] = join(level[i, i + size], level[i + size, i + 2 * size])
        size *= 2
    total[...] = level[0, members].astype(BF16)
    late = pl.ds(DK, DV)

    def to_mate(d, part):
        return remote(
            total.at[:, part], total_got.at[team, :, part], s2.at[d], r2.at[team], {"seq": mates[d - 1]}
        )

    def each_mate(act):
        for d in sorted(range(1, groups), key=lambda d: -min(d, groups - d)):
            pl.when(team == 0)(lambda: act(to_mate(d, late)))
            pl.when((team > 0) & (team + d < groups))(lambda: act(to_mate(d, pl.ds(0, DK + DV))))

    each_mate(lambda copy: copy.start())

    prefix = [None]
    for i in range(1, members):
        size = i & -i
        if i > size:
            level[0, i] = join(level[0, i - size], level[i - size, i])
        prefix.append(level[0, i])
    state = jnp.zeros((DK, DV), F32)
    for i in range(groups - 1):

        @pl.when(team > i)
        def _():
            part = total_got.at[i, :, late] if i == 0 else total_got.at[i]
            remote(part, part, s2.at[0], r2.at[i], {"seq": mates[0]}).wait_recv()

        whole = total_got[i].astype(F32)
        moved = whole[:, DK:]
        if i > 0:
            moved = moved + state - mm(whole[:, :DK].astype(BF16), state.astype(BF16))
        state = jnp.where(team > i, moved, state)
    entry = state
    rounded = entry.astype(BF16)
    start[0] = rounded
    for i in range(1, members):
        begin = entry + prefix[i][:, DK:] - mm(prefix[i][:, :DK].astype(BF16), rounded)
        start[i] = begin.astype(BF16)
    for d in reversed(range(1, members)):
        copy = to_member(start, state_ref, s3, r3, d)
        copy.start()
        sends.append(copy)
    state_ref[slot] = start[slot]
    for d in range(0, members, 2):
        for i in near[max(d, 1) : d + 2]:
            remote(state_ref.at[i], state_ref.at[i], s3.at[0], r3.at[i], {"seq": peers[0]}).wait_recv()
        at = [pl.ds(pl.multiple_of(i * DV, DV), DV) for i in near[d : d + 2]]
        pair = [part_ref[:, c] + mm(ask_ref[:, c], state_ref[i]) for c, i in zip(at, near[d : d + 2])]
        scales = [lax.rsqrt(jnp.mean(x * x, axis=-1, keepdims=True) + eps_norm) for x in pair]
        for c, x, scale in zip(at, pair, scales):
            gated_ref[:, c] = (x * scale * gate_ref[:, c]).astype(BF16)

    load_o.wait()
    gated = gated_ref[...]
    tile = out_ref.shape[1]
    half = rows // 2
    upper, lower = pl.ds(0, half), pl.ds(half, half)

    def share(to):
        columns = pl.ds(pl.multiple_of(to * tile, tile), tile)
        return mm(gated, o_buf[:, columns]).astype(BF16)

    right, far, left = others
    opp[...] = share(far)
    hops = [
        remote(opp.at[upper], hop.at[upper], sr.at[0], rr.at[0], {"head": right}),
        remote(opp.at[lower], hop.at[lower], sr.at[1], rr.at[1], {"head": left}),
    ]
    for copy in hops:
        copy.start()
    to_right, to_left = share(right), share(left)
    keep[upper], keep[lower] = to_right[:half], to_left[half:]
    direct[lower], direct[upper] = to_right[half:], to_left[:half]
    lands = [
        remote(direct.at[lower], land.at[lower], sr.at[2], rr.at[2], {"head": right}),
        remote(direct.at[upper], land.at[upper], sr.at[3], rr.at[3], {"head": left}),
    ]
    for copy in lands:
        copy.start()
    ends = []
    for n, (at, to) in enumerate(((upper, right), (lower, left))):
        hops[n].wait_recv()
        relay[at] = (hop[at].astype(F32) + keep[at].astype(F32)).astype(BF16)
        copy = remote(relay.at[at], hop.at[pl.ds(rows + n * half, half)], sr.at[4 + n], rr.at[4 + n], {"head": to})
        copy.start()
        ends.append(copy)
    mine = share(row_at).astype(F32)
    for n, at in ((1, upper), (0, lower)):
        lands[n].wait_recv()
        ends[1 - n].wait_recv()
        top = 0 if n == 1 else half
        out_ref[at] = (
            mine[top : top + half] + land[at].astype(F32) + hop[pl.ds(rows + top, half)].astype(F32)
        ).astype(BF16)

    edge.wait_send()
    for copy in sends + hops + lands + ends:
        copy.wait_send()
    each_mate(lambda copy: copy.wait_send())


def shards(
    hidden,
    w_query,
    w_key,
    w_value,
    w_gate,
    w_beta,
    conv_query,
    conv_key,
    conv_value,
    norm_gain,
    w_out,
):
    size_seq, size_head = lax.axis_size("seq"), lax.axis_size("head")
    rows, depth = hidden.shape
    wide = w_value.shape[1]
    heads = wide // DV
    groups = size_seq // heads
    tile = w_out.shape[1] // size_head
    vmem = pl.BlockSpec(memory_space=pltpu.VMEM)
    hbm = pl.BlockSpec(memory_space=pl.ANY)
    like = lambda a: pltpu.VMEM(a.shape, a.dtype)
    dma = pltpu.SemaphoreType.DMA
    bufs = [like(a) for a in (hidden, w_query, w_key, w_value, w_gate, w_out)]
    bufs += [pltpu.VMEM((HALO, depth), BF16), dma((6,)), dma, dma]
    rule = [
        pltpu.VMEM((rows, wide), F32),
        pltpu.VMEM((rows, w_key.shape[1]), F32),
        pltpu.VMEM((rows, w_query.shape[1]), F32),
        pltpu.VMEM((rows, wide), F32),
        pltpu.VMEM((rows, wide), BF16),
        pltpu.VMEM((heads, DK, DK + DV), BF16),
        pltpu.VMEM((2 * heads, rows // 2, rows // 2), F32),
        pltpu.VMEM((2 * heads, rows // 2, rows // 2), F32),
        pltpu.VMEM((w_key.shape[1] // DK, rows, DK), F32),
        pltpu.VMEM((rows, heads * DK), F32),
        pltpu.VMEM((heads, rows // 2, rows // 2), BF16),
        pltpu.VMEM((heads, rows, DK + DV), F32),
    ]
    scan = [
        pltpu.VMEM((heads, DK, DK + DV), BF16),
        pltpu.VMEM((DK, DK + DV), BF16),
        pltpu.VMEM((groups, DK, DK + DV), BF16),
        pltpu.VMEM((heads, DK, DV), BF16),
        pltpu.VMEM((heads, DK, DV), BF16),
    ]
    scan += [dma((heads,)), dma((heads,)), dma((groups,)), dma((groups,)), dma((heads,)), dma((heads,))]
    shares = [pltpu.VMEM((rows, wide), F32), pltpu.VMEM((rows, wide), BF16)]
    shares += [pltpu.VMEM((rows, tile), BF16)] * 4
    shares += [pltpu.VMEM((2 * rows, tile), BF16), pltpu.VMEM((rows, tile), BF16), dma((6,)), dma((6,))]
    return pl.pallas_call(
        functools.partial(layer_kernel, (size_seq, size_head, heads)),
        in_specs=[hbm] * 5 + [vmem] * 5 + [hbm],
        out_specs=vmem,
        out_shape=pltpu.VMEM((rows, tile), BF16),
        scratch_shapes=[bufs, rule, scan, shares],
        compiler_params=pltpu.CompilerParams(collective_id=0, has_side_effects=True),
        name="layer",
    )(
        hidden,
        w_query,
        w_key,
        w_value,
        w_gate,
        w_beta.T,
        conv_query,
        conv_key,
        conv_value,
        norm_gain.reshape(1, DV),
        w_out,
    )


def solution(mesh):
    in_specs = (
        P("seq", None),
        P(None, "head"),
        P(None, "head"),
        P(None, "head"),
        P(None, "head"),
        P(None, "head"),
        P(None, "head"),
        P(None, "head"),
        P(None, "head"),
        P(),
        P("head", None),
    )
    out_specs = P("seq", "head")
    return jax.shard_map(shards, mesh=mesh, in_specs=in_specs, out_specs=out_specs, check_vma=False)
```

```python
import functools

import jax
import jax.numpy as jnp
from jax import lax
from jax.experimental import pallas as pl
from jax.experimental.pallas import tpu as pltpu
from jax.sharding import PartitionSpec as P

DK = 128
DV = 128
KER = 4
HALO = 8
FILL = 2
eps_norm = 1e-06
F32 = jnp.float32
BF16 = jnp.bfloat16
MESH = pl.DeviceIdType.MESH


def mm(a, b):
    return jnp.dot(a, b, preferred_element_type=F32)


def mm_nt(a, b):
    return lax.dot_general(a, b, (((1,), (1,)), ((), ())), preferred_element_type=F32)


def mm_tn(a, b):
    return lax.dot_general(a, b, (((0,), (0,)), ((), ())), preferred_element_type=F32)


def sigmoid(x):
    return 0.5 + 0.5 * jnp.tanh(0.5 * x)


def silu(x):
    half = 0.5 * x
    return half + half * jnp.tanh(half)


def unit_rows(x):
    return x * lax.rsqrt(jnp.sum(x * x, axis=-1, keepdims=True) + eps_norm)


def block_solve(sys_ref, x_ref, fill):
    count, n = sys_ref.shape[:2]
    zero = jnp.zeros((), BF16)

    def indices():
        return (
            lax.broadcasted_iota(jnp.int32, (n, n), 0),
            lax.broadcasted_iota(jnp.int32, (n, n), 1),
        )

    def pick(i, size, first, stride):
        lane = lax.broadcasted_iota(jnp.int32, (size, n), 1) // size
        out = jnp.zeros((size, n), F32)
        for b in range(first, n // size, stride):
            out = jnp.where(lane == b - first, sys_ref[i, b * size : (b + 1) * size], out)
        return out

    def spread(x, size, mask):
        return jnp.where(mask, jnp.concatenate([x.astype(BF16)] * (n // size), axis=0), zero)

    def series():
        size = 16
        row, col = indices()
        same = (row // size) == (col // size)
        small = lax.broadcasted_iota(jnp.int32, (size, n), 1) % size
        eye = (small == lax.broadcasted_iota(jnp.int32, (size, n), 0)).astype(F32)
        powers = [-pick(i, size, 0, 1) for i in range(count)]
        solved = [eye + p for p in powers]
        powers = [mm(p.astype(BF16), spread(p, size, same)) for p in powers]
        for last in (False, False, True):
            wide = [spread(p, size, same) for p in powers]
            if last:
                solved = [x + mm(x.astype(BF16), w) for x, w in zip(solved, wide)]
            else:
                both = [
                    mm(jnp.concatenate([x, p], axis=0).astype(BF16), w)
                    for x, p, w in zip(solved, powers, wide)
                ]
                solved = [x + y[:size] for x, y in zip(solved, both)]
                powers = [y[size:] for y in both]
        for i in range(count):
            x_ref[i, :size] = solved[i]
        fill()

    series()
    size = 16
    while size < n:

        def double(size):
            row, col = indices()
            same = (row // size) == (col // size)
            below = ((row // size) == (col // size) + 1) & ((row // size) % 2 == 1)
            odd = (lax.broadcasted_iota(jnp.int32, (size, n), 1) // size) % 2 == 1
            solved = [x_ref[i, :size] for i in range(count)]
            cross = [
                mm(pick(i, size, 1, 2).astype(BF16), spread(x, size, same))
                for i, x in enumerate(solved)
            ]
            cross = [mm(x.astype(BF16), spread(c, size, below)) for x, c in zip(solved, cross)]
            for i in range(count):
                x_ref[i, :size] = jnp.where(odd, 0.0, solved[i])
                x_ref[i, size : 2 * size] = jnp.where(odd, solved[i], -cross[i])
            fill()

        double(size)
        size *= 2


def query_side(queries, kb):
    half = queries[0].shape[0] // 2
    row = lax.broadcasted_iota(jnp.int32, (half, half), 0)
    col = lax.broadcasted_iota(jnp.int32, (half, half), 1)
    masked = []
    for q, k in zip(queries, kb):
        score = mm_nt(q.astype(BF16), k)
        upper = jnp.where(row >= col, score[:half, :half], 0.0).astype(BF16)
        lower = jnp.concatenate(
            [score[half:, :half], jnp.where(row >= col, score[half:, half:], 0.0)], axis=1
        ).astype(BF16)
        masked.append((upper, lower))
    return masked


def value_side(solves, sides):
    half = sides[0].shape[0] // 2
    tops = [mm(x[0], s[:half].astype(BF16)).astype(BF16) for x, s in zip(solves, sides)]
    rest = [(s[half:] - mm(x[2], t)).astype(BF16) for s, x, t in zip(sides, solves, tops)]
    ends = [mm(x[1], r).astype(BF16) for x, r in zip(solves, rest)]
    return [jnp.concatenate(pair, axis=0) for pair in zip(tops, ends)]


def join(first, second):
    return first + second - mm(second[:, :DK].astype(BF16), first.astype(BF16))


def layer_kernel(
    sizes, hid, wq, wk, wv, wg, wb, cq, ck, cv, gain, wo, out_ref, bufs, rule, scan, shares
):
    size_seq, size_head, members = sizes
    groups = size_seq // members
    me, row_at = lax.axis_index("seq"), lax.axis_index("head")
    slot, team = lax.rem(me, members), me // members
    after, before = lax.rem(me + 1, size_seq), lax.rem(me + size_seq - 1, size_seq)
    peers = [team * members + lax.rem(slot + d, members) for d in range(1, members)]
    mates = [lax.rem(team + d, groups) * members + slot for d in range(1, groups)]
    others = [lax.rem(row_at + d, size_head) for d in range(1, size_head)]

    def remote(src, dst, send, recv, to):
        return pltpu.make_async_remote_copy(
            src_ref=src, dst_ref=dst, send_sem=send, recv_sem=recv, device_id=to, device_id_type=MESH
        )

    barrier = pltpu.get_barrier_semaphore()
    greeted = [{"seq": i} for i in [after, before] + peers + mates]
    greeted += [{"head": i} for i in (others[0], others[-1])]
    for to in greeted:
        pl.semaphore_signal(barrier, inc=1, device_id=to, device_id_type=MESH)

    h_buf, q_buf, k_buf, v_buf, g_buf, o_buf, halo, load_sem, edge_send, edge_recv = bufs
    rows = h_buf.shape[0]
    ways = ((hid, h_buf), (wk, k_buf), (wq, q_buf), (wv, v_buf), (wg, g_buf), (wo, o_buf))
    loads = [pltpu.make_async_copy(src, dst, load_sem.at[i]) for i, (src, dst) in enumerate(ways)]
    load_h, load_k, load_q, load_v, load_g, load_o = loads
    for copy in loads[:-2]:
        copy.start()

    pl.semaphore_wait(barrier, len(greeted))

    edge = remote(hid.at[pl.ds(rows - HALO, HALO)], halo, edge_send, edge_recv, {"seq": after})
    edge.start()

    ext_v, ext_k, ext_q, part_ref, ask_ref, carry_ref = rule[:6]
    sys_ref, x_ref, key_ref, beta_ref, corner_ref, side_ref = rule[6:]
    load_h.wait()
    h = h_buf[...]
    beta = 0.05 + 0.15 * sigmoid(mm_nt(h, wb[...]))
    heads = beta.shape[1]
    lane = lax.broadcasted_iota(jnp.int32, (heads, heads * DK), 1) // DK
    ones = (lane == lax.broadcasted_iota(jnp.int32, (heads, heads * DK), 0)).astype(F32).astype(BF16)
    top = beta.astype(BF16)
    beta_ref[...] = mm(top, ones) + mm((beta - top.astype(F32)).astype(BF16), ones)

    def taps_over(x, t):
        summed = t[KER - 1 :] * x
        for n in range(KER - 1):
            summed = summed + t[n : n + 1] * pltpu.roll(x, KER - 1 - n, 0)
        return summed

    def convolve(ext, edge_rows, taps, j):
        at = slice(j * DK, (j + 1) * DK)
        t = 0.5 * taps[:, at].astype(F32)
        body = taps_over(ext[:, at], t)
        brink = jnp.concatenate([edge_rows[:, at], ext[:8, at]], axis=0)
        summed = jnp.concatenate([taps_over(brink, t)[8:], body[8:]], axis=0)
        return summed + summed * jnp.tanh(summed)

    projections = ((load_k, k_buf, ext_k), (load_q, q_buf, ext_q), (load_v, v_buf, ext_v))
    for load, w, ext in projections:
        load.wait()
        ext[...] = mm(h, w[...])
    load_g.start()
    load_o.start()
    edge.wait_recv()
    border = halo[...]
    border = jnp.where(me > 0, border, jnp.zeros_like(border))
    edge_k, edge_q, edge_v = [mm(border, w[...])[HALO - 8 :] for _, w, _ in projections]
    count = k_buf.shape[1] // DK
    group = heads // count
    half = rows // 2
    keys = [unit_rows(convolve(ext_k, edge_k, ck, j)) for j in range(count)]
    kb = [k.astype(BF16) for k in keys]
    row = lax.broadcasted_iota(jnp.int32, (half, half), 0)
    col = lax.broadcasted_iota(jnp.int32, (half, half), 1)
    for n, k in enumerate(kb):
        gram = mm_nt(k, k)
        first = jnp.where(row > col, gram[:half, :half], 0.0)
        last = jnp.where(row > col, gram[half:, half:], 0.0)
        key_ref[n] = keys[n]
        for j in range(n * group, (n + 1) * group):
            b = beta_ref[:, j * DK : (j + 1) * DK]
            sys_ref[2 * j] = b[:half] * first
            sys_ref[2 * j + 1] = b[half:] * last
            corner_ref[j] = (b[half:] * gram[half:, :half]).astype(BF16)
    done = []

    def fill():
        for j in range(len(done), min(len(done) + FILL, heads)):
            b = beta_ref[:, j * DK : (j + 1) * DK]
            side_ref[j, :, :DK] = b * key_ref[j // group]
            side_ref[j, :, DK:] = b * convolve(ext_v, edge_v, cv, j)
            done.append(j)

    block_solve(sys_ref, x_ref, fill)
    while len(done) < heads:
        fill()
    solves = [
        (x_ref[2 * j].astype(BF16), x_ref[2 * j + 1].astype(BF16), corner_ref[j])
        for j in range(heads)
    ]
    sides = [side_ref[j] for j in range(heads)]

    got, total, total_got, start, state_ref, s1, r1, s2, r2, s3, r3 = scan

    turns = [(n * members // 4, c) for n in (0, 1, 3, 2) for c in range(members // 4)]
    near = [
        lax.rem(slot - lax.rem(slot, members // 4) + n, members) + lax.rem(slot + c, members // 4)
        for n, c in turns
    ]

    def to_member(src, dst, send, recv, d):
        return remote(
            src.at[near[d]], dst.at[slot], send.at[d], recv.at[slot], {"seq": team * members + near[d]}
        )

    sends = []
    sides = value_side(solves, sides)
    for j, side in enumerate(sides):
        carry_ref[j] = mm_tn(kb[j // group], side).astype(BF16)
    for d in reversed(range(1, members)):
        copy = to_member(carry_ref, got, s1, r1, d)
        copy.start()
        sends.append(copy)
    got[slot] = carry_ref[slot]

    queries = [unit_rows(convolve(ext_q, edge_q, cq, j)) for j in range(count)]
    masked = query_side(queries, kb)
    for j, side in enumerate(sides):
        at = slice(j * DV, (j + 1) * DV)
        upper, lower = masked[j // group]
        seen = jnp.concatenate([mm(upper, side[:half]), mm(lower, side)], axis=0)
        part_ref[:, at] = seen[:, DK:]
        ask_ref[:, at] = (queries[j // group] - seen[:, :DK]).astype(BF16)
    gate_ref, gated_ref, keep, relay, opp, direct, hop, land, sr, rr = shares
    spans = []
    for i in range(members):

        @pl.when(slot != i)
        def _():
            remote(got.at[i], got.at[i], s1.at[0], r1.at[i], {"seq": peers[0]}).wait_recv()

        spans.append(got[i].astype(F32))
    level = {(i, i + 1): x for i, x in enumerate(spans)}
    size = 1
    while size < members:
        for i in range(0, members, 2 * size):
            level[i, i + 2 * size] = join(level[i, i + size], level[i + size, i + 2 * size])
        size *= 2
    total[...] = level[0, members].astype(BF16)
    late = pl.ds(DK, DV)

    def to_mate(d, part):
        return remote(
            total.at[:, part], total_got.at[team, :, part], s2.at[d], r2.at[team], {"seq": mates[d - 1]}
        )

    def each_mate(act):
        for d in sorted(range(1, groups), key=lambda d: -min(d, groups - d)):
            pl.when(team == 0)(lambda: act(to_mate(d, late)))
            pl.when((team > 0) & (team + d < groups))(lambda: act(to_mate(d, pl.ds(0, DK + DV))))

    each_mate(lambda copy: copy.start())

    load_g.wait()
    gain_row = gain[...].astype(F32)
    gate = silu(mm(h, g_buf[...]).astype(BF16).astype(F32))
    for j in range(heads):
        at = slice(j * DV, (j + 1) * DV)
        gate_ref[:, at] = gate[:, at] * gain_row

    prefix = [None]
    for i in range(1, members):
        size = i & -i
        if i > size:
            level[0, i] = join(level[0, i - size], level[i - size, i])
        prefix.append(level[0, i])
    state = jnp.zeros((DK, DV), F32)
    for i in range(groups - 1):

        @pl.when(team > i)
        def _():
            part = total_got.at[i, :, late] if i == 0 else total_got.at[i]
            remote(part, part, s2.at[0], r2.at[i], {"seq": mates[0]}).wait_recv()

        whole = total_got[i].astype(F32)
        moved = whole[:, DK:]
        if i > 0:
            moved = moved + state - mm(whole[:, :DK].astype(BF16), state.astype(BF16))
        state = jnp.where(team > i, moved, state)
    entry = state
    rounded = entry.astype(BF16)
    start[0] = rounded
    for i in range(1, members):
        begin = entry + prefix[i][:, DK:] - mm(prefix[i][:, :DK].astype(BF16), rounded)
        start[i] = begin.astype(BF16)
    for d in reversed(range(1, members)):
        copy = to_member(start, state_ref, s3, r3, d)
        copy.start()
        sends.append(copy)
    state_ref[slot] = start[slot]
    for d in range(0, members, 2):
        for i in near[max(d, 1) : d + 2]:
            remote(state_ref.at[i], state_ref.at[i], s3.at[0], r3.at[i], {"seq": peers[0]}).wait_recv()
        at = [pl.ds(pl.multiple_of(i * DV, DV), DV) for i in near[d : d + 2]]
        pair = [part_ref[:, c] + mm(ask_ref[:, c], state_ref[i]) for c, i in zip(at, near[d : d + 2])]
        scales = [lax.rsqrt(jnp.mean(x * x, axis=-1, keepdims=True) + eps_norm) for x in pair]
        for c, x, scale in zip(at, pair, scales):
            gated_ref[:, c] = (x * scale * gate_ref[:, c]).astype(BF16)

    load_o.wait()
    gated = gated_ref[...]
    tile = out_ref.shape[1]
    half = rows // 2
    upper, lower = pl.ds(0, half), pl.ds(half, half)

    def share(to):
        columns = pl.ds(pl.multiple_of(to * tile, tile), tile)
        return mm(gated, o_buf[:, columns]).astype(BF16)

    right, far, left = others
    opp[...] = share(far)
    hops = [
        remote(opp.at[upper], hop.at[upper], sr.at[0], rr.at[0], {"head": right}),
        remote(opp.at[lower], hop.at[lower], sr.at[1], rr.at[1], {"head": left}),
    ]
    for copy in hops:
        copy.start()
    to_right, to_left = share(right), share(left)
    keep[upper], keep[lower] = to_right[:half], to_left[half:]
    direct[lower], direct[upper] = to_right[half:], to_left[:half]
    lands = [
        remote(direct.at[lower], land.at[lower], sr.at[2], rr.at[2], {"head": right}),
        remote(direct.at[upper], land.at[upper], sr.at[3], rr.at[3], {"head": left}),
    ]
    for copy in lands:
        copy.start()
    ends = []
    for n, (at, to) in enumerate(((upper, right), (lower, left))):
        hops[n].wait_recv()
        relay[at] = (hop[at].astype(F32) + keep[at].astype(F32)).astype(BF16)
        copy = remote(relay.at[at], hop.at[pl.ds(rows + n * half, half)], sr.at[4 + n], rr.at[4 + n], {"head": to})
        copy.start()
        ends.append(copy)
    mine = share(row_at).astype(F32)
    for n, at in ((1, upper), (0, lower)):
        lands[n].wait_recv()
        ends[1 - n].wait_recv()
        top = 0 if n == 1 else half
        out_ref[at] = (
            mine[top : top + half] + land[at].astype(F32) + hop[pl.ds(rows + top, half)].astype(F32)
        ).astype(BF16)

    edge.wait_send()
    for copy in sends + hops + lands + ends:
        copy.wait_send()
    each_mate(lambda copy: copy.wait_send())


def shards(
    hidden,
    w_query,
    w_key,
    w_value,
    w_gate,
    w_beta,
    conv_query,
    conv_key,
    conv_value,
    norm_gain,
    w_out,
):
    size_seq, size_head = lax.axis_size("seq"), lax.axis_size("head")
    rows, depth = hidden.shape
    wide = w_value.shape[1]
    heads = wide // DV
    groups = size_seq // heads
    tile = w_out.shape[1] // size_head
    vmem = pl.BlockSpec(memory_space=pltpu.VMEM)
    hbm = pl.BlockSpec(memory_space=pl.ANY)
    like = lambda a: pltpu.VMEM(a.shape, a.dtype)
    dma = pltpu.SemaphoreType.DMA
    bufs = [like(a) for a in (hidden, w_query, w_key, w_value, w_gate, w_out)]
    bufs += [pltpu.VMEM((HALO, depth), BF16), dma((6,)), dma, dma]
    rule = [
        pltpu.VMEM((rows, wide), F32),
        pltpu.VMEM((rows, w_key.shape[1]), F32),
        pltpu.VMEM((rows, w_query.shape[1]), F32),
        pltpu.VMEM((rows, wide), F32),
        pltpu.VMEM((rows, wide), BF16),
        pltpu.VMEM((heads, DK, DK + DV), BF16),
        pltpu.VMEM((2 * heads, rows // 2, rows // 2), F32),
        pltpu.VMEM((2 * heads, rows // 2, rows // 2), F32),
        pltpu.VMEM((w_key.shape[1] // DK, rows, DK), F32),
        pltpu.VMEM((rows, heads * DK), F32),
        pltpu.VMEM((heads, rows // 2, rows // 2), BF16),
        pltpu.VMEM((heads, rows, DK + DV), F32),
    ]
    scan = [
        pltpu.VMEM((heads, DK, DK + DV), BF16),
        pltpu.VMEM((DK, DK + DV), BF16),
        pltpu.VMEM((groups, DK, DK + DV), BF16),
        pltpu.VMEM((heads, DK, DV), BF16),
        pltpu.VMEM((heads, DK, DV), BF16),
    ]
    scan += [dma((heads,)), dma((heads,)), dma((groups,)), dma((groups,)), dma((heads,)), dma((heads,))]
    shares = [pltpu.VMEM((rows, wide), F32), pltpu.VMEM((rows, wide), BF16)]
    shares += [pltpu.VMEM((rows, tile), BF16)] * 4
    shares += [pltpu.VMEM((2 * rows, tile), BF16), pltpu.VMEM((rows, tile), BF16), dma((6,)), dma((6,))]
    return pl.pallas_call(
        functools.partial(layer_kernel, (size_seq, size_head, heads)),
        in_specs=[hbm] * 5 + [vmem] * 5 + [hbm],
        out_specs=vmem,
        out_shape=pltpu.VMEM((rows, tile), BF16),
        scratch_shapes=[bufs, rule, scan, shares],
        compiler_params=pltpu.CompilerParams(collective_id=0, has_side_effects=True),
        name="layer",
    )(
        hidden,
        w_query,
        w_key,
        w_value,
        w_gate,
        w_beta.T,
        conv_query,
        conv_key,
        conv_value,
        norm_gain.reshape(1, DV),
        w_out,
    )


def solution(mesh):
    in_specs = (
        P("seq", None),
        P(None, "head"),
        P(None, "head"),
        P(None, "head"),
        P(None, "head"),
        P(None, "head"),
        P(None, "head"),
        P(None, "head"),
        P(None, "head"),
        P(),
        P("head", None),
    )
    out_specs = P("seq", "head")
    return jax.shard_map(shards, mesh=mesh, in_specs=in_specs, out_specs=out_specs, check_vma=False)
```
